256 devices in a mesh: clip: 32 (over x, z_hi, core), tile: 8 (over y, z_lo).
Axes of the slice: x: 4, y: 4, z: 8 (z_hi: 4, z_lo: 2; z = z_hi * 2 + z_lo), core: 2. Of those that a mesh axis runs over, the one named last changes fastest.
Arguments:
- latents: bfloat16 [64, 40, 64, 320], P('clip', 'tile'), may hold values from -64 to 64
- lengths: int32 [32], P('clip'), may hold values from 1 to 2, as said below
- context: int32 [8], replicated, may hold values from 0 to 63, as said below
- gain_first: float32 [320], replicated, may hold values from 0.25 to 1.75
- conv_first: bfloat16 [3, 3, 320, 320], replicated, may hold values from -0.109375 to 0.109375
- gain_second: float32 [320], replicated, may hold values from 0.25 to 1.75
- conv_second: bfloat16 [3, 3, 320, 320], replicated, may hold values from -0.109375 to 0.109375
- time_weight: bfloat16 [3, 320, 320], replicated, may hold values from -0.1875 to 0.1875
- attn_gain: float32 [320], replicated, may hold values from 0.25 to 1.75
- w_qkv: bfloat16 [320, 960], replicated, may hold values from -2 to 2
- w_out: bfloat16 [320, 320], replicated, may hold values from -0.3125 to 0.3125
Outputs:
- block_out: bfloat16 [64, 40, 64, 320], P('clip', 'tile')
The draws below stay inside these ranges and needn't reach their ends.
Inputs may be any that keep to these rules, and one draw needn't show every extreme that they name: `lengths`: the last clip is full with 2 live frames and some other clip has 1. The context frames lie in distinct clips; each names slot c * 2 + f of a live frame f < lengths[c].
All inputs are finite; a program needn't handle non-finite values.
Results may differ from the reference program's by a relative error of at most 0.011.
Values may be sent and summed in bfloat16 or wider, within the bound.
A program may use at most 64 MiB of HBM per device.

```python
import math
import jax
import jax.numpy as jnp
from jax import lax

C = 320
HEAD_DIM = 64
GROUPS = 32
H = 40
W = 64
F_CAP = 2
NCTX = 8
CLIPS = 32
FRAMES = 64


def clip_plan(key):
    base_key = jax.random.fold_in(key, 101)
    key_len, key_half, key_clip, key_slot = jax.random.split(base_key, 4)
    half_cap = F_CAP // 2
    counts = half_cap + jax.random.randint(key_len, (CLIPS,), 0, F_CAP - half_cap + 1)
    half_clip = 1 + jax.random.randint(key_half, (), 0, CLIPS - 2)
    counts = counts.at[CLIPS - 1].set(F_CAP).at[half_clip].set(half_cap)
    middle = 1 + jax.random.permutation(key_clip, CLIPS - 2)[:NCTX - 2]
    chosen = jnp.concatenate([jnp.zeros((1,), jnp.int32), middle.astype(jnp.int32), jnp.full((1,), CLIPS - 1, jnp.int32)])
    offsets = jax.random.randint(key_slot, (NCTX,), 0, F_CAP) % counts[chosen]
    offsets = offsets.at[0].set(0).at[NCTX - 1].set(F_CAP - 1)
    return (counts.astype(jnp.int32), (chosen * F_CAP + offsets).astype(jnp.int32))


def draw_lengths(key, part):
    return clip_plan(key)[0]


def draw_context(key, part):
    return clip_plan(key)[1]


def draw_latents(key, part):
    key_noise, key_chan, key_row, key_frame = jax.random.split(jax.random.fold_in(key, 202), 4)
    shape_full = (FRAMES, H, W, C)
    noise = jnp.clip(jax.random.normal(key_noise, shape_full), -4.0, 4.0)
    channel_scale = jnp.exp(jax.random.uniform(key_chan, (C,), minval=math.log(0.3), maxval=math.log(3.0)))
    rising = 3.0 ** (jnp.arange(H).astype(jnp.float32) / (H - 1))
    row_scale = rising * jax.random.uniform(key_row, (H,), minval=0.7, maxval=1.4) / 1.7
    frame_scale = jnp.exp(jax.random.uniform(key_frame, (FRAMES,), minval=math.log(0.5), maxval=math.log(2.0)))
    values = noise * frame_scale[:, None, None, None] * row_scale[None, :, None, None] * channel_scale
    return jnp.clip(values, -64.0, 64.0).astype(jnp.bfloat16)


def draw_w_qkv(key, part):
    key_base = jax.random.fold_in(jax.random.fold_in(key, 303), 0)
    weights = jnp.clip(jax.random.normal(key_base, (C, 3 * C)), -6.0, 6.0) * C ** (-0.5)
    return jnp.clip(weights, -2.0, 2.0).astype(jnp.bfloat16)


def centred(key, extent, deviation, limit, held_as=jnp.bfloat16):
    values = deviation * jax.random.normal(key, extent, jnp.float32)
    return jnp.clip(values, min=-limit, max=limit).astype(held_as)


def setup_inputs(seed: int = 0) -> dict:
    seeds = jax.random.split(jax.random.key(seed), 12)
    latents = draw_latents(jax.random.fold_in(seeds[11], 71), 0)
    lengths = draw_lengths(jax.random.fold_in(seeds[11], 71), 0)
    context = draw_context(jax.random.fold_in(seeds[11], 71), 0)
    gain_first = jnp.clip(1.0 + 0.15 * jax.random.normal(seeds[3], (C,), jnp.float32), 0.25, 1.75)
    conv_first = centred(seeds[4], (3, 3, C, C), (9 * C) ** -0.5, 0.109375)
    gain_second = jnp.clip(1.0 + 0.15 * jax.random.normal(seeds[5], (C,), jnp.float32), 0.25, 1.75)
    conv_second = centred(seeds[6], (3, 3, C, C), (9 * C) ** -0.5, 0.109375)
    time_weight = centred(seeds[7], (3, C, C), (3 * C) ** -0.5, 0.1875)
    attn_gain = jnp.clip(1.0 + 0.15 * jax.random.normal(seeds[8], (C,), jnp.float32), 0.25, 1.75)
    w_qkv = draw_w_qkv(jax.random.fold_in(seeds[11], 71), 0)
    w_out = centred(seeds[10], (C, C), C ** -0.5, 0.3125)
    return {"latents": latents, "lengths": lengths, "context": context, "gain_first": gain_first, "conv_first": conv_first, "gain_second": gain_second, "conv_second": conv_second, "time_weight": time_weight, "attn_gain": attn_gain, "w_qkv": w_qkv, "w_out": w_out}


EPS = 1e-05
MASKED = -1e+30

def group_sums(source):
    frame_count, row_count, col_count, channels = source.shape
    group_width = channels // GROUPS
    values = source.astype(jnp.float32).reshape(frame_count, row_count * col_count, GROUPS, group_width)
    return (lax.optimization_barrier(jnp.sum(values, axis=(1, 3))), lax.optimization_barrier(jnp.sum(values * values, axis=(1, 3))))

def finish(total_sum, square_sum, gain):
    group_width = gain.shape[0] // GROUPS
    count = H * W * group_width
    centre = total_sum / count
    spread = square_sum / count - centre * centre
    inverse = lax.rsqrt(spread + EPS)
    scale = jnp.repeat(inverse, group_width, axis=1) * gain[None, :]
    shift = -jnp.repeat(centre, group_width, axis=1) * scale
    return (scale, shift)

def activate(source, scale, shift):
    return jax.nn.silu(source.astype(jnp.float32) * scale[:, None, None, :] + shift[:, None, None, :]).astype(jnp.bfloat16)

def convolve(padded, weights):
    wide = jnp.pad(padded, ((0, 0), (0, 0), (1, 1), (0, 0)))
    row_count = padded.shape[1] - 2
    col_count = padded.shape[2]
    result = jnp.zeros((padded.shape[0], row_count, col_count, weights.shape[-1]), jnp.float32)
    for row_step in range(3):
        for col_step in range(3):
            window = wide[:, row_step:row_step + row_count, col_step:col_step + col_count, :]
            result = result + jnp.dot(window, weights[row_step, col_step], preferred_element_type=jnp.float32)
    return result

def conv_clips(activated, weights):
    blocks = activated.reshape(CLIPS, F_CAP, H, W, C)

    def one_clip(block):
        return convolve(jnp.pad(block, ((0, 0), (1, 1), (0, 0), (0, 0))), weights)
    return lax.map(one_clip, blocks).reshape(FRAMES, H, W, C)

def layer_norm(source, gain):
    values = source.astype(jnp.float32)
    centre = lax.optimization_barrier(jnp.mean(values, axis=-1, keepdims=True))
    spread = lax.optimization_barrier(jnp.mean((values - centre) ** 2, axis=-1, keepdims=True))
    return ((values - centre) * lax.rsqrt(spread + EPS) * gain).astype(jnp.bfloat16)

def attend(packed, shared_kv, live_count):
    frame_count, cell_count, packed_width = packed.shape
    channels = packed_width // 3
    head_count = channels // HEAD_DIM
    shape_local = (frame_count, cell_count, head_count, HEAD_DIM)
    shape_shared = (shared_kv.shape[0], cell_count, head_count, HEAD_DIM)
    queries = packed[..., :channels].reshape(shape_local).astype(jnp.float32)
    keys_local = packed[..., channels:2 * channels].reshape(shape_local).astype(jnp.float32)
    values_local = packed[..., 2 * channels:].reshape(shape_local).astype(jnp.float32)
    keys_shared = shared_kv[..., :channels].reshape(shape_shared).astype(jnp.float32)
    values_shared = shared_kv[..., channels:].reshape(shape_shared).astype(jnp.float32)
    score_scale = HEAD_DIM ** (-0.5)
    near_scores = jnp.einsum('fnhd,gnhd->nhfg', queries, keys_local) * score_scale
    visible = jnp.arange(frame_count) < live_count
    near_scores = jnp.where(visible, near_scores, MASKED)
    far_scores = jnp.einsum('fnhd,jnhd->nhfj', queries, keys_shared) * score_scale
    ceiling = jnp.maximum(lax.optimization_barrier(jnp.max(near_scores, axis=-1)), lax.optimization_barrier(jnp.max(far_scores, axis=-1)))[..., None]
    near_exp = jnp.exp(near_scores - ceiling)
    far_exp = jnp.exp(far_scores - ceiling)
    normaliser = lax.optimization_barrier(jnp.sum(near_exp, axis=-1, keepdims=True)) + lax.optimization_barrier(jnp.sum(far_exp, axis=-1, keepdims=True))
    near_weight = (near_exp / normaliser).astype(jnp.bfloat16).astype(jnp.float32)
    far_weight = (far_exp / normaliser).astype(jnp.bfloat16).astype(jnp.float32)
    result = jnp.einsum('nhfg,gnhd->fnhd', near_weight, values_local)
    result = result + jnp.einsum('nhfj,jnhd->fnhd', far_weight, values_shared)
    return result.reshape(frame_count, cell_count, channels).astype(jnp.bfloat16)

def reference(latents, lengths, context, gain_first, conv_first, gain_second, conv_second, time_weight, attn_gain, w_qkv, w_out):
    total_sum, square_sum = group_sums(latents)
    scale, shift = finish(total_sum, square_sum, gain_first)
    hidden_one = conv_clips(activate(latents, scale, shift), conv_first).astype(jnp.bfloat16)
    total_sum, square_sum = group_sums(hidden_one)
    scale, shift = finish(total_sum, square_sum, gain_second)
    res_one = (latents.astype(jnp.float32) + conv_clips(activate(hidden_one, scale, shift), conv_second)).astype(jnp.bfloat16)
    res_one = res_one.reshape(CLIPS, F_CAP, H, W, C)
    moving = jax.nn.silu(res_one.astype(jnp.float32)).astype(jnp.bfloat16)
    clip_ids = jnp.arange(CLIPS).astype(jnp.int32)
    final_frames = moving[clip_ids, (lengths - 1).astype(jnp.int32)]
    prior = jnp.concatenate([jnp.zeros_like(final_frames[:1]), final_frames[:-1]], axis=0)
    later = jnp.concatenate([moving[1:, 0], jnp.zeros_like(final_frames[:1])], axis=0)
    backward = jnp.concatenate([prior[:, None], moving[:, :-1]], axis=1)
    forward = jnp.concatenate([moving[:, 1:], jnp.zeros_like(moving[:, :1])], axis=1)
    slots = jnp.arange(F_CAP).astype(jnp.int32)
    at_end = (slots[None, :] == lengths[:, None] - 1)[:, :, None, None, None]
    forward = jnp.where(at_end, later[:, None], forward)
    mixed = res_one.astype(jnp.float32) + jnp.dot(backward, time_weight[0], preferred_element_type=jnp.float32)
    mixed = mixed + jnp.dot(moving, time_weight[1], preferred_element_type=jnp.float32)
    mixed = mixed + jnp.dot(forward, time_weight[2], preferred_element_type=jnp.float32)
    res_two = mixed.astype(jnp.bfloat16)
    normed = layer_norm(res_two, attn_gain).reshape(CLIPS, F_CAP, H * W, C)

    def project_clip(block):
        return jnp.dot(block, w_qkv, preferred_element_type=jnp.float32).astype(jnp.bfloat16)
    packed = lax.map(project_clip, normed)
    pairs = packed[..., C:].reshape(FRAMES, H * W, 2 * C)
    shared_kv = jnp.take(pairs, context, axis=0)

    def attend_clip(item):
        return attend(item[0], shared_kv, item[1])
    attended = lax.map(attend_clip, (packed, lengths))
    result = res_two.astype(jnp.float32).reshape(CLIPS, F_CAP, H * W, C)
    result = result + jnp.dot(attended, w_out, preferred_element_type=jnp.float32)
    live = (slots[None, :] < lengths[:, None])[:, :, None, None]
    result = jnp.where(live, result, 0.0)
    return result.astype(jnp.bfloat16).reshape(FRAMES, H, W, C)
```

```python
import jax
import jax.numpy as jnp
from jax import lax
from jax.experimental import pallas as pl
from jax.experimental.pallas import tpu as pltpu
from jax.sharding import PartitionSpec as P

MESH = pl.DeviceIdType.MESH
F32 = jnp.float32
BF16 = jnp.bfloat16

C = 320
HEAD_DIM = 64
HEADS = 5
GROUP_WIDTH = 10
H = 40
W = 64
ROWS = 5
CLIPS = 32
TILES = 8
COUNT = H * W * GROUP_WIDTH
EPS = 1e-05
MASKED = -1e30
DEAD = 1e30
DEAD_LIMIT = 1e20
CHUNKS = ((0, 3), (3, 2))


def dot(a, b):
    return jnp.dot(a, b, preferred_element_type=F32)


def silu(y):
    half = 0.5 * y
    return half + half * jnp.tanh(half)


def rounded(v):
    return v.astype(BF16).astype(F32)


def channel_sums(frames):
    sums = [jnp.sum(v, axis=0, keepdims=True) for v in frames]
    squares = [jnp.sum(v * v, axis=0, keepdims=True) for v in frames]
    return jnp.concatenate(sums + squares + [jnp.zeros((4, C), F32)], axis=0)


def kernel(
    lat, length, context, gain_one, gain_two, gain_attn,
    w_one_hbm, w_two_hbm, w_time_hbm, w_qkv_hbm, w_out_hbm,
    out,
    w_one, w_two, w_time, w_qkv, w_out,
    taps, hid, halo, stat_send, stat_recv, packed, spread,
    send_0, send_1, recv_0, recv_1, back_send_0, back_send_1, back_recv_0, back_recv_1,
    load_sem, halo_send_sem, halo_recv_sem, stat_send_sem, stat_recv_sem,
    a2a_send_sem, a2a_recv_sem,
):
    clip = lax.axis_index("clip")
    tile = lax.axis_index("tile")
    tile_up = lax.rem(tile + TILES - 1, TILES)
    tile_down = lax.rem(tile + 1, TILES)

    barrier = pltpu.get_barrier_semaphore()

    def greet_tile(i, carry):
        pl.semaphore_signal(
            barrier, inc=1, device_id={"tile": lax.rem(tile + i, TILES)}, device_id_type=MESH
        )
        return carry

    def greet_clip(i, carry):
        pl.semaphore_signal(
            barrier, inc=1, device_id={"clip": lax.rem(clip + i, CLIPS)}, device_id_type=MESH
        )
        return carry

    lax.fori_loop(1, TILES, greet_tile, 0)
    lax.fori_loop(1, CLIPS, greet_clip, 0)

    loads = [
        pltpu.make_async_copy(source, target, load_sem.at[i])
        for i, (source, target) in enumerate(
            (
                (w_one_hbm, w_one),
                (w_two_hbm, w_two),
                (w_time_hbm, w_time),
                (w_qkv_hbm, w_qkv),
                (w_out_hbm, w_out),
            )
        )
    ]
    for load in loads:
        load.start()

    first = channel_sums([lat[0].astype(F32), lat[1].astype(F32)])
    stat_send[0] = first
    pl.semaphore_wait(barrier, TILES - 1 + CLIPS - 1)

    def halo_copies(phase, source):
        low = pltpu.make_async_remote_copy(
            src_ref=source.at[:, pl.ds((ROWS - 1) * W, W)],
            dst_ref=halo.at[phase, 0],
            send_sem=halo_send_sem.at[phase, 0],
            recv_sem=halo_recv_sem.at[phase, 0],
            device_id={"tile": tile_down},
            device_id_type=MESH,
        )
        high = pltpu.make_async_remote_copy(
            src_ref=source.at[:, pl.ds(0, W)],
            dst_ref=halo.at[phase, 1],
            send_sem=halo_send_sem.at[phase, 1],
            recv_sem=halo_recv_sem.at[phase, 1],
            device_id={"tile": tile_up},
            device_id_type=MESH,
        )
        return low, high

    def stat_copy(phase, peer, slot):
        return pltpu.make_async_remote_copy(
            src_ref=stat_send.at[phase],
            dst_ref=stat_recv.at[phase, slot],
            send_sem=stat_send_sem.at[phase, peer],
            recv_sem=stat_recv_sem.at[phase, slot],
            device_id={"tile": peer},
            device_id_type=MESH,
        )

    def exchange_start(phase, source):
        def send(i, carry):
            stat_copy(phase, lax.rem(tile + i, TILES), tile).start()
            return carry

        lax.fori_loop(1, TILES, send, 0)
        for copy in halo_copies(phase, source):
            copy.start()

    def exchange_finish(phase, source, own, gain):
        def arrive(i, carry):
            peer = lax.rem(tile + i, TILES)
            stat_copy(phase, peer, peer).wait_recv()
            return carry

        lax.fori_loop(1, TILES, arrive, 0)
        stat_recv[phase, tile] = own
        total = stat_recv[phase, 0]
        for i in range(1, TILES):
            total = total + stat_recv[phase, i]
        rows = lax.broadcasted_iota(jnp.int32, (C, C), 0)
        cols = lax.broadcasted_iota(jnp.int32, (C, C), 1)
        member = ((rows * 6554) >> 16) == ((cols * 6554) >> 16)
        grouped = jnp.dot(
            total,
            jnp.where(member, 1.0, 0.0).astype(F32),
            precision=lax.Precision.HIGHEST,
            preferred_element_type=F32,
        ) * (1.0 / COUNT)
        centre = grouped[0:2]
        variance = grouped[2:4] - centre * centre
        scale = lax.rsqrt(variance + EPS) * gain[...]
        shift = -centre * scale
        for copy in halo_copies(phase, source):
            copy.wait_recv()
        return scale, shift

    def exchange_drain(phase, source):
        def drain(i, carry):
            stat_copy(phase, lax.rem(tile + i, TILES), tile).wait_send()
            return carry

        lax.fori_loop(1, TILES, drain, 0)
        for copy in halo_copies(phase, source):
            copy.wait_send()

    def put_taps(f, start, rows, value, scale, shift, keep=None):
        a = silu(value.astype(F32) * scale + shift)
        if keep is not None:
            a = jnp.where(keep, a, 0.0)
        column = lax.broadcasted_iota(jnp.int32, (rows * W, C), 0) & (W - 1)
        before = jnp.where(column == 0, 0.0, pltpu.roll(a, 1, 0))
        after = jnp.where(column == W - 1, 0.0, pltpu.roll(a, rows * W - 1, 0))
        taps[f, pl.ds(start, rows * W), :] = jnp.concatenate(
            [before.astype(BF16), a.astype(BF16), after.astype(BF16)], axis=1
        )

    def fill_taps(phase, source, scale, shift):
        for f in range(2):
            sc, sh = scale[f : f + 1], shift[f : f + 1]
            put_taps(f, W, ROWS, source[f], sc, sh)
            put_taps(f, 0, 1, halo[phase, 0, f], sc, sh, tile > 0)
            put_taps(f, (ROWS + 1) * W, 1, halo[phase, 1, f], sc, sh, tile < TILES - 1)

    def convolve(f, row, rows, weights):
        total = dot(taps[f, pl.ds(row * W, rows * W), :], weights[0])
        for a in (1, 2):
            total = total + dot(taps[f, pl.ds((row + a) * W, rows * W), :], weights[a])
        return total

    exchange_start(0, lat)
    scale, shift = exchange_finish(0, lat, first, gain_one)
    fill_taps(0, lat, scale, shift)
    loads[0].wait()
    frames = []
    for f in range(2):
        value = convolve(f, 0, ROWS, w_one).astype(BF16)
        hid[f] = value
        frames.append(value.astype(F32))
    second = channel_sums(frames)
    stat_send[1] = second

    exchange_start(1, hid)
    exchange_drain(0, lat)
    scale, shift = exchange_finish(1, hid, second, gain_two)
    fill_taps(1, hid, scale, shift)
    loads[1].wait()

    def a2a_copy(way, chunk, source, target, peer, slot):
        return pltpu.make_async_remote_copy(
            src_ref=source.at[peer],
            dst_ref=target.at[slot],
            send_sem=a2a_send_sem.at[way, chunk, peer],
            recv_sem=a2a_recv_sem.at[way, chunk, slot],
            device_id={"clip": peer},
            device_id_type=MESH,
        )

    def pack_row(r, value):
        base = r * 10 * CLIPS
        packed[pl.ds(base, 128), :] = value[:, 0:128]
        packed[pl.ds(base + 128, 128), :] = value[:, 128:256]
        packed[pl.ds(base + 256, 64), :] = jnp.concatenate(
            [value[0:64, 256:320], value[64:128, 256:320]], axis=1
        )

    def a2a_start(way, chunk, source, target):
        row, rows = CHUNKS[chunk]
        depth = rows * 10

        def pick(peer):
            return packed[pl.ds(row * 10 * CLIPS + peer, depth, stride=CLIPS), :].astype(BF16)

        def stage(i, carry):
            peer = lax.rem(clip + i, CLIPS)
            source[peer] = pick(peer)
            return carry

        def send(i, carry):
            peer = lax.rem(clip + i, CLIPS)
            a2a_copy(way, chunk, source, target, peer, clip).start()
            return carry

        lax.fori_loop(1, CLIPS, stage, 0)
        target[clip] = pick(clip)
        lax.fori_loop(1, CLIPS, send, 0)

    def a2a_finish(way, chunk, source, target):
        rows = CHUNKS[chunk][1]
        depth = rows * 10

        def arrive(i, carry):
            peer = lax.rem(clip + i, CLIPS)
            a2a_copy(way, chunk, source, target, peer, peer).wait_recv()
            return carry

        lax.fori_loop(1, CLIPS, arrive, 0)

        def widen(i, carry):
            spread[pl.ds(pl.multiple_of(i * 32, 32), depth), :] = target[i].astype(F32)
            return carry

        lax.fori_loop(0, CLIPS, widen, 0)
        return [unpack_row(q) for q in range(rows)]

    def a2a_drain(way, chunk, source, target):
        def drain(i, carry):
            peer = lax.rem(clip + i, CLIPS)
            a2a_copy(way, chunk, source, target, peer, clip).wait_send()
            return carry

        lax.fori_loop(1, CLIPS, drain, 0)

    def unpack_row(q):
        def column(k):
            return spread[pl.ds(q * 10 + k, CLIPS, stride=32), :]

        left = jnp.concatenate([column(k) for k in range(4)], axis=0)
        middle = jnp.concatenate([column(4 + k) for k in range(4)], axis=0)
        tail = jnp.concatenate([column(8), column(9)], axis=0)
        right = jnp.concatenate([tail, pltpu.roll(tail, 64, 1)], axis=0)
        return jnp.concatenate([left, middle, right[:, 0:64]], axis=1)

    one_live = length[0] == 1
    sends, recvs = (send_0, send_1), (recv_0, recv_1)
    back_sends, back_recvs = (back_send_0, back_send_1), (back_recv_0, back_recv_1)

    for chunk, (row, rows) in enumerate(CHUNKS):
        halves = []
        for f in range(2):
            value = lat[f, pl.ds(row * W, rows * W), :].astype(F32) + convolve(f, row, rows, w_two)
            if f == 1:
                value = jnp.where(one_live, DEAD, value)
            halves.append(value)
        for q in range(rows):
            span = slice(q * W, (q + 1) * W)
            pack_row(row + q, jnp.concatenate([halves[0][span], halves[1][span]], axis=0))
        a2a_start(0, chunk, sends[chunk], recvs[chunk])

    for load in loads[2:]:
        load.wait()
    exchange_drain(1, hid)

    lane = lax.broadcasted_iota(jnp.int32, (128, 128), 1)
    line = lax.broadcasted_iota(jnp.int32, (128, 128), 0)
    lane_clip, lane_cell, lane_slot = lane & 31, (lane >> 5) & 1, lane >> 6
    line_clip, line_cell = line & 31, (line >> 5) & 1
    lane_frame = lane_clip * 2 + lane_slot
    shared = jnp.zeros((128, 128), F32)
    for j in range(8):
        shared = shared + jnp.where(lane_frame == context[j], 1.0, 0.0)
    low_half = lane < HEAD_DIM
    clip_row = lax.broadcasted_iota(jnp.int32, (CLIPS, C), 0)

    for chunk, (row, rows) in enumerate(CHUNKS):
        blocks = a2a_finish(0, chunk, sends[chunk], recvs[chunk])
        dead = jnp.broadcast_to(blocks[0][64:96, 0:1], (CLIPS, 128)) > DEAD_LIMIT
        dead_wide = jnp.broadcast_to(blocks[0][64:96, 0:1], (CLIPS, C)) > DEAD_LIMIT
        dead_f = jnp.where(dead, 1.0, 0.0)
        dead_lane = jnp.sum(
            jnp.where(
                lax.broadcasted_iota(jnp.int32, (CLIPS, 128), 0)
                == (lax.broadcasted_iota(jnp.int32, (CLIPS, 128), 1) & 31),
                dead_f,
                0.0,
            ),
            axis=0,
            keepdims=True,
        )
        live_key = 1.0 - jnp.where(lane_slot == 1, jnp.broadcast_to(dead_lane, (128, 128)), 0.0)
        weight = jnp.where(
            lane_cell == line_cell,
            jnp.where(lane_clip == line_clip, live_key, 0.0) + shared,
            0.0,
        )
        visible = weight > 0.0
        weight2 = jnp.concatenate([weight, weight], axis=1)
        visible2 = jnp.concatenate([visible, visible], axis=1)

        sources = []
        for q in range(rows):
            x = jnp.where(blocks[q] > DEAD_LIMIT, 0.0, blocks[q])
            sources.append(x)
            moving = rounded(silu(x))
            before, after = [None] * 4, [None] * 4
            for cell in range(2):
                m0 = moving[cell * 32 : cell * 32 + 32]
                m1 = moving[64 + cell * 32 : 96 + cell * 32]
                final = jnp.where(dead_wide, m0, m1)
                prior = jnp.where(clip_row == 0, 0.0, pltpu.roll(final, 1, 0))
                later = jnp.where(clip_row == CLIPS - 1, 0.0, pltpu.roll(m0, CLIPS - 1, 0))
                before[cell], before[2 + cell] = prior, m0
                after[cell], after[2 + cell] = jnp.where(dead_wide, later, m1), later
            taps[0, pl.ds(q * 128, 128), :] = jnp.concatenate(
                [
                    jnp.concatenate(before, axis=0).astype(BF16),
                    moving.astype(BF16),
                    jnp.concatenate(after, axis=0).astype(BF16),
                ],
                axis=1,
            )
        source = jnp.concatenate(sources, axis=0)
        res_two = rounded(source + dot(taps[0, pl.ds(0, rows * 128), :], w_time[...]))
        centre = jnp.mean(res_two, axis=1, keepdims=True)
        offset = res_two - centre
        variance = jnp.mean(offset * offset, axis=1, keepdims=True)
        normed = (offset * lax.rsqrt(variance + EPS) * gain_attn[...]).astype(BF16)
        q_all = dot(normed, w_qkv[:, 0:C]).astype(BF16)
        k_all = dot(normed, w_qkv[:, C : 2 * C]).astype(BF16)
        v_all = dot(normed, w_qkv[:, 2 * C : 3 * C]).astype(BF16)
        zero = jnp.zeros((128, 128), BF16)
        attended = []
        for q in range(rows):
            span = slice(q * 128, (q + 1) * 128)
            pieces = []
            for pair in range(2):
                cols = slice(pair * 128, (pair + 1) * 128)
                queries, keys, values = q_all[span, cols], k_all[span, cols], v_all[span, cols]
                keys2 = jnp.concatenate(
                    [jnp.where(low_half, keys, zero), jnp.where(low_half, zero, keys)], axis=0
                )
                values2 = jnp.concatenate(
                    [jnp.where(low_half, values, zero), jnp.where(low_half, zero, values)], axis=0
                )
                scores = lax.dot_general(
                    queries, keys2, (((1,), (1,)), ((), ())), preferred_element_type=F32
                ) * (HEAD_DIM**-0.5)
                scores = jnp.where(visible2, scores, MASKED)
                top = jnp.concatenate(
                    [
                        jnp.broadcast_to(
                            jnp.max(scores[:, i * 128 : (i + 1) * 128], axis=1, keepdims=True),
                            (128, 128),
                        )
                        for i in range(2)
                    ],
                    axis=1,
                )
                grown = jnp.exp(scores - top) * weight2
                norm = jnp.where(
                    low_half,
                    jnp.broadcast_to(jnp.sum(grown[:, 0:128], axis=1, keepdims=True), (128, 128)),
                    jnp.broadcast_to(jnp.sum(grown[:, 128:256], axis=1, keepdims=True), (128, 128)),
                )
                pieces.append((dot(grown.astype(BF16), values2) / norm).astype(BF16))
            cols = slice(256, 320)
            scores = lax.dot_general(
                q_all[span, cols], k_all[span, cols], (((1,), (1,)), ((), ())),
                preferred_element_type=F32,
            ) * (HEAD_DIM**-0.5)
            scores = jnp.where(visible, scores, MASKED)
            grown = jnp.exp(scores - jnp.max(scores, axis=1, keepdims=True)) * weight
            norm = jnp.sum(grown, axis=1, keepdims=True)
            pieces.append((dot(grown.astype(BF16), v_all[span, cols]) / norm).astype(BF16))
            attended.append(jnp.concatenate(pieces, axis=1))
        result = res_two + dot(jnp.concatenate(attended, axis=0), w_out[...])
        for q in range(rows):
            block = result[q * 128 : (q + 1) * 128]
            parts = [block[0:64]]
            for cell in range(2):
                parts.append(jnp.where(dead_wide, 0.0, block[64 + cell * 32 : 96 + cell * 32]))
            pack_row(row + q, jnp.concatenate(parts, axis=0))
        a2a_start(1, chunk, back_sends[chunk], back_recvs[chunk])

    for chunk in range(2):
        a2a_drain(0, chunk, sends[chunk], recvs[chunk])
    for chunk, (row, rows) in enumerate(CHUNKS):
        blocks = a2a_finish(1, chunk, back_sends[chunk], back_recvs[chunk])
        for q in range(rows):
            for f in range(2):
                out[f, pl.ds((row + q) * W, W), :] = blocks[q][f * 64 : (f + 1) * 64].astype(BF16)
    for chunk in range(2):
        a2a_drain(1, chunk, back_sends[chunk], back_recvs[chunk])


def local(
    latents, lengths, context, gain_first, conv_first, gain_second, conv_second,
    time_weight, attn_gain, w_qkv, w_out,
):
    vmem = pl.BlockSpec(memory_space=pltpu.VMEM)
    smem = pl.BlockSpec(memory_space=pltpu.SMEM)
    hbm = pl.BlockSpec(memory_space=pl.ANY)

    def messages(chunk):
        return pltpu.VMEM((CLIPS, CHUNKS[chunk][1] * 10, 128), BF16)

    result = pl.pallas_call(
        kernel,
        out_shape=jax.ShapeDtypeStruct((2, ROWS * W, C), BF16),
        in_specs=[vmem, smem, smem, vmem, vmem, vmem, hbm, hbm, hbm, hbm, hbm],
        out_specs=vmem,
        scratch_shapes=[
            pltpu.VMEM((3, 3 * C, C), BF16),
            pltpu.VMEM((3, 3 * C, C), BF16),
            pltpu.VMEM((3 * C, C), BF16),
            pltpu.VMEM((C, 3 * C), BF16),
            pltpu.VMEM((C, C), BF16),
            pltpu.VMEM((2, (ROWS + 2) * W, 3 * C), BF16),
            pltpu.VMEM((2, ROWS * W, C), BF16),
            pltpu.VMEM((2, 2, 2, W, C), BF16),
            pltpu.VMEM((2, 8, C), F32),
            pltpu.VMEM((2, TILES, 8, C), F32),
            pltpu.VMEM((ROWS * 10 * CLIPS, 128), F32),
            pltpu.VMEM((CLIPS * 32, 128), F32),
            messages(0), messages(1), messages(0), messages(1),
            messages(0), messages(1), messages(0), messages(1),
            pltpu.SemaphoreType.DMA((5,)),
            pltpu.SemaphoreType.DMA((2, 2)),
            pltpu.SemaphoreType.DMA((2, 2)),
            pltpu.SemaphoreType.DMA((2, TILES)),
            pltpu.SemaphoreType.DMA((2, TILES)),
            pltpu.SemaphoreType.DMA((2, 2, CLIPS)),
            pltpu.SemaphoreType.DMA((2, 2, CLIPS)),
        ],
        compiler_params=pltpu.CompilerParams(
            collective_id=0, has_side_effects=True, vmem_limit_bytes=48 << 20
        ),
        name="block",
    )(
        latents.reshape(2, ROWS * W, C),
        lengths,
        context,
        gain_first.reshape(1, C),
        gain_second.reshape(1, C),
        attn_gain.reshape(1, C),
        conv_first.reshape(3, 3 * C, C),
        conv_second.reshape(3, 3 * C, C),
        time_weight.reshape(3 * C, C),
        w_qkv,
        w_out,
    )
    return result.reshape(2, ROWS, W, C)


def solution(mesh):
    placed = (P("clip", "tile", None, None), P("clip"), P(), P(), P(), P(), P(), P(), P(), P(), P())
    return jax.shard_map(
        local, mesh=mesh, in_specs=placed, out_specs=P("clip", "tile", None, None), check_vma=False
    )
```

```python
import jax
import jax.numpy as jnp
from jax import lax
from jax.experimental import pallas as pl
from jax.experimental.pallas import tpu as pltpu
from jax.sharding import PartitionSpec as P

MESH = pl.DeviceIdType.MESH
F32 = jnp.float32
BF16 = jnp.bfloat16

C = 320
HEAD_DIM = 64
HEADS = 5
GROUP_WIDTH = 10
H = 40
W = 64
ROWS = 5
CLIPS = 32
TILES = 8
COUNT = H * W * GROUP_WIDTH
EPS = 1e-05
MASKED = -1e30
DEAD = 1e30
DEAD_LIMIT = 1e20
CHUNKS = ((0, 3), (3, 2))


def dot(a, b):
    return jnp.dot(a, b, preferred_element_type=F32)


def silu(y):
    half = 0.5 * y
    return half + half * jnp.tanh(half)


def rounded(v):
    return v.astype(BF16).astype(F32)


def channel_sums(frames):
    sums = [jnp.sum(v, axis=0, keepdims=True) for v in frames]
    squares = [jnp.sum(v * v, axis=0, keepdims=True) for v in frames]
    return jnp.concatenate(sums + squares + [jnp.zeros((4, C), F32)], axis=0)


def kernel(
    lat_hbm, length, context, gain_one, gain_two, gain_attn,
    w_one_hbm, w_two_hbm, w_time_hbm, w_qkv_hbm, w_out_hbm,
    out,
    lat, w_one, w_two, w_time, w_qkv, w_out,
    taps, hid, halo, stat_send, stat_recv, packed, spread,
    send_0, send_1, recv_0, recv_1, back_send_0, back_send_1, back_recv_0, back_recv_1,
    load_sem, halo_send_sem, halo_recv_sem, stat_send_sem, stat_recv_sem,
    a2a_send_sem, a2a_recv_sem,
):
    clip = lax.axis_index("clip")
    tile = lax.axis_index("tile")
    tile_up = lax.rem(tile + TILES - 1, TILES)
    tile_down = lax.rem(tile + 1, TILES)

    loads = [
        pltpu.make_async_copy(source, target, load_sem.at[i])
        for i, (source, target) in enumerate(
            (
                (lat_hbm, lat),
                (w_one_hbm, w_one),
                (w_two_hbm, w_two),
                (w_time_hbm, w_time),
                (w_qkv_hbm, w_qkv),
                (w_out_hbm, w_out),
            )
        )
    ]
    for load in loads:
        load.start()

    barrier = pltpu.get_barrier_semaphore()

    def greet_tile(i, carry):
        pl.semaphore_signal(
            barrier, inc=1, device_id={"tile": lax.rem(tile + i, TILES)}, device_id_type=MESH
        )
        return carry

    def greet_clip(i, carry):
        pl.semaphore_signal(
            barrier, inc=1, device_id={"clip": lax.rem(clip + i, CLIPS)}, device_id_type=MESH
        )
        return carry

    lax.fori_loop(1, TILES, greet_tile, 0)
    lax.fori_loop(1, CLIPS, greet_clip, 0)

    loads[0].wait()
    first = channel_sums([lat[0].astype(F32), lat[1].astype(F32)])
    stat_send[0] = first
    pl.semaphore_wait(barrier, TILES - 1 + CLIPS - 1)

    def halo_copies(phase, source):
        low = pltpu.make_async_remote_copy(
            src_ref=source.at[:, pl.ds((ROWS - 1) * W, W)],
            dst_ref=halo.at[phase, 0],
            send_sem=halo_send_sem.at[phase, 0],
            recv_sem=halo_recv_sem.at[phase, 0],
            device_id={"tile": tile_down},
            device_id_type=MESH,
        )
        high = pltpu.make_async_remote_copy(
            src_ref=source.at[:, pl.ds(0, W)],
            dst_ref=halo.at[phase, 1],
            send_sem=halo_send_sem.at[phase, 1],
            recv_sem=halo_recv_sem.at[phase, 1],
            device_id={"tile": tile_up},
            device_id_type=MESH,
        )
        return low, high

    def stat_copy(phase, peer, slot):
        return pltpu.make_async_remote_copy(
            src_ref=stat_send.at[phase],
            dst_ref=stat_recv.at[phase, slot],
            send_sem=stat_send_sem.at[phase, peer],
            recv_sem=stat_recv_sem.at[phase, slot],
            device_id={"tile": peer},
            device_id_type=MESH,
        )

    def exchange_start(phase, source):
        def send(i, carry):
            stat_copy(phase, lax.rem(tile + i, TILES), tile).start()
            return carry

        lax.fori_loop(1, TILES, send, 0)
        for copy in halo_copies(phase, source):
            copy.start()

    def exchange_finish(phase, source, own, gain):
        def arrive(i, carry):
            peer = lax.rem(tile + i, TILES)
            stat_copy(phase, peer, peer).wait_recv()
            return carry

        lax.fori_loop(1, TILES, arrive, 0)
        stat_recv[phase, tile] = own
        total = stat_recv[phase, 0]
        for i in range(1, TILES):
            total = total + stat_recv[phase, i]
        rows = lax.broadcasted_iota(jnp.int32, (C, C), 0)
        cols = lax.broadcasted_iota(jnp.int32, (C, C), 1)
        member = ((rows * 6554) >> 16) == ((cols * 6554) >> 16)
        grouped = jnp.dot(
            total,
            jnp.where(member, 1.0, 0.0).astype(F32),
            precision=lax.Precision.HIGHEST,
            preferred_element_type=F32,
        ) * (1.0 / COUNT)
        centre = grouped[0:2]
        variance = grouped[2:4] - centre * centre
        scale = lax.rsqrt(variance + EPS) * gain[...].reshape(1, C)
        shift = -centre * scale
        for copy in halo_copies(phase, source):
            copy.wait_recv()
        return scale, shift

    def exchange_drain(phase, source):
        def drain(i, carry):
            stat_copy(phase, lax.rem(tile + i, TILES), tile).wait_send()
            return carry

        lax.fori_loop(1, TILES, drain, 0)
        for copy in halo_copies(phase, source):
            copy.wait_send()

    def put_taps(f, start, rows, value, scale, shift, keep=None):
        a = silu(value.astype(F32) * scale + shift)
        if keep is not None:
            a = jnp.where(keep, a, 0.0)
        column = lax.broadcasted_iota(jnp.int32, (rows * W, C), 0) & (W - 1)
        before = jnp.where(column == 0, 0.0, pltpu.roll(a, 1, 0))
        after = jnp.where(column == W - 1, 0.0, pltpu.roll(a, rows * W - 1, 0))
        taps[f, pl.ds(start, rows * W), :] = jnp.concatenate(
            [before.astype(BF16), a.astype(BF16), after.astype(BF16)], axis=1
        )

    def fill_taps(phase, source, scale, shift):
        for f in range(2):
            sc, sh = scale[f : f + 1], shift[f : f + 1]
            put_taps(f, W, ROWS, source[f], sc, sh)
            put_taps(f, 0, 1, halo[phase, 0, f], sc, sh, tile > 0)
            put_taps(f, (ROWS + 1) * W, 1, halo[phase, 1, f], sc, sh, tile < TILES - 1)

    def convolve(f, row, rows, weights):
        total = dot(taps[f, pl.ds(row * W, rows * W), :], weights[0])
        for a in (1, 2):
            total = total + dot(taps[f, pl.ds((row + a) * W, rows * W), :], weights[a])
        return total

    exchange_start(0, lat)
    scale, shift = exchange_finish(0, lat, first, gain_one)
    fill_taps(0, lat, scale, shift)
    loads[1].wait()
    frames = []
    for f in range(2):
        value = convolve(f, 0, ROWS, w_one).astype(BF16)
        hid[f] = value
        frames.append(value.astype(F32))
    second = channel_sums(frames)
    stat_send[1] = second

    exchange_start(1, hid)
    exchange_drain(0, lat)
    scale, shift = exchange_finish(1, hid, second, gain_two)
    fill_taps(1, hid, scale, shift)
    loads[2].wait()

    def a2a_copy(way, chunk, source, target, peer, slot):
        return pltpu.make_async_remote_copy(
            src_ref=source.at[peer],
            dst_ref=target.at[slot],
            send_sem=a2a_send_sem.at[way, chunk, peer],
            recv_sem=a2a_recv_sem.at[way, chunk, slot],
            device_id={"clip": peer},
            device_id_type=MESH,
        )

    def pack_row(r, value):
        base = r * 10 * CLIPS
        packed[pl.ds(base, 128), :] = value[:, 0:128]
        packed[pl.ds(base + 128, 128), :] = value[:, 128:256]
        packed[pl.ds(base + 256, 64), :] = jnp.concatenate(
            [value[0:64, 256:320], value[64:128, 256:320]], axis=1
        )

    def a2a_start(way, chunk, source, target):
        row, rows = CHUNKS[chunk]
        depth = rows * 10

        def pick(peer):
            return packed[pl.ds(row * 10 * CLIPS + peer, depth, stride=CLIPS), :].astype(BF16)

        def stage(i, carry):
            peer = lax.rem(clip + i, CLIPS)
            source[peer] = pick(peer)
            return carry

        def send(i, carry):
            peer = lax.rem(clip + i, CLIPS)
            a2a_copy(way, chunk, source, target, peer, clip).start()
            return carry

        lax.fori_loop(1, CLIPS, stage, 0)
        target[clip] = pick(clip)
        lax.fori_loop(1, CLIPS, send, 0)

    def a2a_finish(way, chunk, source, target):
        rows = CHUNKS[chunk][1]
        depth = rows * 10

        def arrive(i, carry):
            peer = lax.rem(clip + i, CLIPS)
            a2a_copy(way, chunk, source, target, peer, peer).wait_recv()
            return carry

        lax.fori_loop(1, CLIPS, arrive, 0)

        def widen(i, carry):
            spread[pl.ds(pl.multiple_of(i * 32, 32), depth), :] = target[i].astype(F32)
            return carry

        lax.fori_loop(0, CLIPS, widen, 0)
        return [unpack_row(q) for q in range(rows)]

    def a2a_drain(way, chunk, source, target):
        def drain(i, carry):
            peer = lax.rem(clip + i, CLIPS)
            a2a_copy(way, chunk, source, target, peer, clip).wait_send()
            return carry

        lax.fori_loop(1, CLIPS, drain, 0)

    def unpack_row(q):
        def column(k):
            return spread[pl.ds(q * 10 + k, CLIPS, stride=32), :]

        left = jnp.concatenate([column(k) for k in range(4)], axis=0)
        middle = jnp.concatenate([column(4 + k) for k in range(4)], axis=0)
        tail = jnp.concatenate([column(8), column(9)], axis=0)
        right = jnp.concatenate([tail, pltpu.roll(tail, 64, 1)], axis=0)
        return jnp.concatenate([left, middle, right[:, 0:64]], axis=1)

    one_live = length[0] == 1
    sends, recvs = (send_0, send_1), (recv_0, recv_1)
    back_sends, back_recvs = (back_send_0, back_send_1), (back_recv_0, back_recv_1)

    for chunk, (row, rows) in enumerate(CHUNKS):
        halves = []
        for f in range(2):
            value = lat[f, pl.ds(row * W, rows * W), :].astype(F32) + convolve(f, row, rows, w_two)
            if f == 1:
                value = jnp.where(one_live, DEAD, value)
            halves.append(value)
        for q in range(rows):
            span = slice(q * W, (q + 1) * W)
            pack_row(row + q, jnp.concatenate([halves[0][span], halves[1][span]], axis=0))
        a2a_start(0, chunk, sends[chunk], recvs[chunk])

    for load in loads[3:]:
        load.wait()
    exchange_drain(1, hid)

    lane = lax.broadcasted_iota(jnp.int32, (128, 128), 1)
    line = lax.broadcasted_iota(jnp.int32, (128, 128), 0)
    lane_clip, lane_cell, lane_slot = lane & 31, (lane >> 5) & 1, lane >> 6
    line_clip, line_cell = line & 31, (line >> 5) & 1
    lane_frame = lane_clip * 2 + lane_slot
    shared = jnp.zeros((128, 128), F32)
    for j in range(8):
        shared = shared + jnp.where(lane_frame == context[j], 1.0, 0.0)
    low_half = lane < HEAD_DIM
    clip_row = lax.broadcasted_iota(jnp.int32, (CLIPS, C), 0)

    for chunk, (row, rows) in enumerate(CHUNKS):
        blocks = a2a_finish(0, chunk, sends[chunk], recvs[chunk])
        dead = jnp.broadcast_to(blocks[0][64:96, 0:1], (CLIPS, 128)) > DEAD_LIMIT
        dead_wide = jnp.broadcast_to(blocks[0][64:96, 0:1], (CLIPS, C)) > DEAD_LIMIT
        dead_f = jnp.where(dead, 1.0, 0.0)
        dead_lane = jnp.sum(
            jnp.where(
                lax.broadcasted_iota(jnp.int32, (CLIPS, 128), 0)
                == (lax.broadcasted_iota(jnp.int32, (CLIPS, 128), 1) & 31),
                dead_f,
                0.0,
            ),
            axis=0,
            keepdims=True,
        )
        live_key = 1.0 - jnp.where(lane_slot == 1, jnp.broadcast_to(dead_lane, (128, 128)), 0.0)
        weight = jnp.where(
            lane_cell == line_cell,
            jnp.where(lane_clip == line_clip, live_key, 0.0) + shared,
            0.0,
        )
        visible = weight > 0.0
        weight2 = jnp.concatenate([weight, weight], axis=1)
        visible2 = jnp.concatenate([visible, visible], axis=1)

        sources = []
        for q in range(rows):
            x = jnp.where(blocks[q] > DEAD_LIMIT, 0.0, blocks[q])
            sources.append(x)
            moving = rounded(silu(x))
            before, after = [None] * 4, [None] * 4
            for cell in range(2):
                m0 = moving[cell * 32 : cell * 32 + 32]
                m1 = moving[64 + cell * 32 : 96 + cell * 32]
                final = jnp.where(dead_wide, m0, m1)
                prior = jnp.where(clip_row == 0, 0.0, pltpu.roll(final, 1, 0))
                later = jnp.where(clip_row == CLIPS - 1, 0.0, pltpu.roll(m0, CLIPS - 1, 0))
                before[cell], before[2 + cell] = prior, m0
                after[cell], after[2 + cell] = jnp.where(dead_wide, later, m1), later
            taps[0, pl.ds(q * 128, 128), :] = jnp.concatenate(
                [
                    jnp.concatenate(before, axis=0).astype(BF16),
                    moving.astype(BF16),
                    jnp.concatenate(after, axis=0).astype(BF16),
                ],
                axis=1,
            )
        source = jnp.concatenate(sources, axis=0)
        res_two = rounded(source + dot(taps[0, pl.ds(0, rows * 128), :], w_time[...]))
        centre = jnp.mean(res_two, axis=1, keepdims=True)
        offset = res_two - centre
        variance = jnp.mean(offset * offset, axis=1, keepdims=True)
        normed = (offset * lax.rsqrt(variance + EPS) * gain_attn[...].reshape(1, C)).astype(BF16)
        q_all = dot(normed, w_qkv[:, 0:C]).astype(BF16)
        k_all = dot(normed, w_qkv[:, C : 2 * C]).astype(BF16)
        v_all = dot(normed, w_qkv[:, 2 * C : 3 * C]).astype(BF16)
        zero = jnp.zeros((128, 128), BF16)
        attended = []
        for q in range(rows):
            span = slice(q * 128, (q + 1) * 128)
            pieces = []
            for pair in range(2):
                cols = slice(pair * 128, (pair + 1) * 128)
                queries, keys, values = q_all[span, cols], k_all[span, cols], v_all[span, cols]
                keys2 = jnp.concatenate(
                    [jnp.where(low_half, keys, zero), jnp.where(low_half, zero, keys)], axis=0
                )
                values2 = jnp.concatenate(
                    [jnp.where(low_half, values, zero), jnp.where(low_half, zero, values)], axis=0
                )
                scores = lax.dot_general(
                    queries, keys2, (((1,), (1,)), ((), ())), preferred_element_type=F32
                ) * (HEAD_DIM**-0.5)
                scores = jnp.where(visible2, scores, MASKED)
                top = jnp.concatenate(
                    [
                        jnp.broadcast_to(
                            jnp.max(scores[:, i * 128 : (i + 1) * 128], axis=1, keepdims=True),
                            (128, 128),
                        )
                        for i in range(2)
                    ],
                    axis=1,
                )
                grown = jnp.exp(scores - top) * weight2
                norm = jnp.where(
                    low_half,
                    jnp.broadcast_to(jnp.sum(grown[:, 0:128], axis=1, keepdims=True), (128, 128)),
                    jnp.broadcast_to(jnp.sum(grown[:, 128:256], axis=1, keepdims=True), (128, 128)),
                )
                pieces.append((dot(grown.astype(BF16), values2) / norm).astype(BF16))
            cols = slice(256, 320)
            scores = lax.dot_general(
                q_all[span, cols], k_all[span, cols], (((1,), (1,)), ((), ())),
                preferred_element_type=F32,
            ) * (HEAD_DIM**-0.5)
            scores = jnp.where(visible, scores, MASKED)
            grown = jnp.exp(scores - jnp.max(scores, axis=1, keepdims=True)) * weight
            norm = jnp.sum(grown, axis=1, keepdims=True)
            pieces.append((dot(grown.astype(BF16), v_all[span, cols]) / norm).astype(BF16))
            attended.append(jnp.concatenate(pieces, axis=1))
        result = res_two + dot(jnp.concatenate(attended, axis=0), w_out[...])
        for q in range(rows):
            block = result[q * 128 : (q + 1) * 128]
            parts = [block[0:64]]
            for cell in range(2):
                parts.append(jnp.where(dead_wide, 0.0, block[64 + cell * 32 : 96 + cell * 32]))
            pack_row(row + q, jnp.concatenate(parts, axis=0))
        a2a_start(1, chunk, back_sends[chunk], back_recvs[chunk])

    for chunk in range(2):
        a2a_drain(0, chunk, sends[chunk], recvs[chunk])
    for chunk, (row, rows) in enumerate(CHUNKS):
        blocks = a2a_finish(1, chunk, back_sends[chunk], back_recvs[chunk])
        for q in range(rows):
            for f in range(2):
                out[f, pl.ds((row + q) * W, W), :] = blocks[q][f * 64 : (f + 1) * 64].astype(BF16)
    for chunk in range(2):
        a2a_drain(1, chunk, back_sends[chunk], back_recvs[chunk])


def local(
    latents, lengths, context, gain_first, conv_first, gain_second, conv_second,
    time_weight, attn_gain, w_qkv, w_out,
):
    vmem = pl.BlockSpec(memory_space=pltpu.VMEM)
    smem = pl.BlockSpec(memory_space=pltpu.SMEM)
    hbm = pl.BlockSpec(memory_space=pl.ANY)

    def messages(chunk):
        return pltpu.VMEM((CLIPS, CHUNKS[chunk][1] * 10, 128), BF16)

    result = pl.pallas_call(
        kernel,
        out_shape=jax.ShapeDtypeStruct((2, ROWS * W, C), BF16),
        in_specs=[hbm, smem, smem, vmem, vmem, vmem, hbm, hbm, hbm, hbm, hbm],
        out_specs=vmem,
        scratch_shapes=[
            pltpu.VMEM((2, ROWS * W, C), BF16),
            pltpu.VMEM((3, 3 * C, C), BF16),
            pltpu.VMEM((3, 3 * C, C), BF16),
            pltpu.VMEM((3 * C, C), BF16),
            pltpu.VMEM((C, 3 * C), BF16),
            pltpu.VMEM((C, C), BF16),
            pltpu.VMEM((2, (ROWS + 2) * W, 3 * C), BF16),
            pltpu.VMEM((2, ROWS * W, C), BF16),
            pltpu.VMEM((2, 2, 2, W, C), BF16),
            pltpu.VMEM((2, 8, C), F32),
            pltpu.VMEM((2, TILES, 8, C), F32),
            pltpu.VMEM((ROWS * 10 * CLIPS, 128), F32),
            pltpu.VMEM((CLIPS * 32, 128), F32),
            messages(0), messages(1), messages(0), messages(1),
            messages(0), messages(1), messages(0), messages(1),
            pltpu.SemaphoreType.DMA((6,)),
            pltpu.SemaphoreType.DMA((2, 2)),
            pltpu.SemaphoreType.DMA((2, 2)),
            pltpu.SemaphoreType.DMA((2, TILES)),
            pltpu.SemaphoreType.DMA((2, TILES)),
            pltpu.SemaphoreType.DMA((2, 2, CLIPS)),
            pltpu.SemaphoreType.DMA((2, 2, CLIPS)),
        ],
        compiler_params=pltpu.CompilerParams(
            collective_id=0, has_side_effects=True, vmem_limit_bytes=67043328
        ),
        name="block",
    )(
        latents.reshape(2, ROWS * W, C),
        lengths,
        context,
        gain_first,
        gain_second,
        attn_gain,
        conv_first.reshape(3, 3 * C, C),
        conv_second.reshape(3, 3 * C, C),
        time_weight.reshape(3 * C, C),
        w_qkv,
        w_out,
    )
    return result.reshape(2, ROWS, W, C)


def solution(mesh):
    placed = (P("clip", "tile", None, None), P("clip"), P(), P(), P(), P(), P(), P(), P(), P(), P())
    return jax.shard_map(
        local, mesh=mesh, in_specs=placed, out_specs=P("clip", "tile", None, None), check_vma=False
    )
```

```python
import jax
import jax.numpy as jnp
from jax import lax
from jax.experimental import pallas as pl
from jax.experimental.pallas import tpu as pltpu
from jax.sharding import PartitionSpec as P

MESH = pl.DeviceIdType.MESH
F32 = jnp.float32
BF16 = jnp.bfloat16

C = 320
HEAD_DIM = 64
HEADS = 5
GROUP_WIDTH = 10
H = 40
W = 64
ROWS = 5
CLIPS = 32
TILES = 8
COUNT = H * W * GROUP_WIDTH
EPS = 1e-05
MASKED = -1e30
DEAD = 1e30
DEAD_LIMIT = 1e20
CHUNKS = ((1, 2, 3), (0, 4))
STARTS = (0, 3)


def dot(a, b):
    return jnp.dot(a, b, preferred_element_type=F32)


def silu(y):
    half = 0.5 * y
    return half + half * jnp.tanh(half)


def rounded(v):
    return v.astype(BF16).astype(F32)


def channel_sums(frames):
    sums = [jnp.sum(v, axis=0, keepdims=True) for v in frames]
    squares = [jnp.sum(v * v, axis=0, keepdims=True) for v in frames]
    return jnp.concatenate(sums + squares, axis=0)


def kernel(
    lat_hbm, length, context, gain_one, gain_two, gain_attn,
    w_one_hbm, w_two_hbm, w_time_hbm, w_qkv_hbm, w_out_hbm,
    out,
    lat, w_one, w_two, w_time, w_qkv, w_out,
    taps, hid, halo_send, halo, member, stat_send, stat_recv, packed, spread,
    send_0, send_1, recv_0, recv_1, back_send_0, back_send_1, back_recv_0, back_recv_1,
    load_sem, halo_send_sem, halo_recv_sem, stat_send_sem, stat_recv_sem,
    a2a_send_sem, a2a_recv_sem,
):
    clip = lax.axis_index("clip")
    tile = lax.axis_index("tile")
    tile_up = lax.rem(tile + TILES - 1, TILES)
    tile_down = lax.rem(tile + 1, TILES)

    loads = [
        pltpu.make_async_copy(source, target, load_sem.at[i])
        for i, (source, target) in enumerate(
            (
                (lat_hbm, lat),
                (w_one_hbm, w_one),
                (w_two_hbm, w_two),
                (w_time_hbm, w_time),
                (w_qkv_hbm, w_qkv),
                (w_out_hbm, w_out),
            )
        )
    ]
    for load in loads:
        load.start()

    barrier = pltpu.get_barrier_semaphore()

    def greet_tile(i, carry):
        pl.semaphore_signal(
            barrier, inc=1, device_id={"tile": lax.rem(tile + i, TILES)}, device_id_type=MESH
        )
        return carry

    def greet_clip(i, carry):
        pl.semaphore_signal(
            barrier, inc=1, device_id={"clip": lax.rem(clip + i, CLIPS)}, device_id_type=MESH
        )
        return carry

    lax.fori_loop(1, TILES, greet_tile, 0)
    lax.fori_loop(1, CLIPS, greet_clip, 0)

    rows = lax.broadcasted_iota(jnp.int32, (C, C), 0)
    cols = lax.broadcasted_iota(jnp.int32, (C, C), 1)
    member[...] = jnp.where(((rows * 6554) >> 16) == ((cols * 6554) >> 16), 1.0, 0.0).astype(BF16)

    def pack_halo(phase, source):
        for way, start in enumerate(((ROWS - 1) * W, 0)):
            span = pl.ds(start, W)
            for f in range(2):
                halo_send[phase, way, 2 * f] = source[f, span, 0:128]
                halo_send[phase, way, 2 * f + 1] = source[f, span, 128:256]
            halo_send[phase, way, 4] = jnp.concatenate(
                [source[0, span, 256:320], source[1, span, 256:320]], axis=1
            )

    loads[0].wait()
    pack_halo(0, lat)
    first = channel_sums([lat[0].astype(F32), lat[1].astype(F32)])
    stat_send[0] = first
    pl.semaphore_wait(barrier, TILES - 1 + CLIPS - 1)

    def halo_copies(phase):
        return [
            pltpu.make_async_remote_copy(
                src_ref=halo_send.at[phase, way],
                dst_ref=halo.at[phase, way],
                send_sem=halo_send_sem.at[phase, way],
                recv_sem=halo_recv_sem.at[phase, way],
                device_id={"tile": peer},
                device_id_type=MESH,
            )
            for way, peer in enumerate((tile_down, tile_up))
        ]

    def stat_copy(phase, peer, slot):
        return pltpu.make_async_remote_copy(
            src_ref=stat_send.at[phase],
            dst_ref=stat_recv.at[phase, slot],
            send_sem=stat_send_sem.at[phase, peer],
            recv_sem=stat_recv_sem.at[phase, slot],
            device_id={"tile": peer},
            device_id_type=MESH,
        )

    def stats_start(phase):
        def send(i, carry):
            stat_copy(phase, lax.rem(tile + i, TILES), tile).start()
            return carry

        lax.fori_loop(1, TILES, send, 0)

    def halo_start(phase):
        for copy in halo_copies(phase):
            copy.start()

    def halo_finish(phase):
        for copy in halo_copies(phase):
            copy.wait_recv()

    def stats_finish(phase, own, gain):
        stat_recv[phase, tile] = own

        def arrive(i, carry):
            peer = lax.rem(tile + i, TILES)
            stat_copy(phase, peer, peer).wait_recv()
            return carry

        lax.fori_loop(1, TILES, arrive, 0)
        total = stat_recv[phase, 0]
        for i in range(1, TILES):
            total = total + stat_recv[phase, i]
        top = total.astype(BF16)
        rest = total - top.astype(F32)
        mid = rest.astype(BF16)
        low = (rest - mid.astype(F32)).astype(BF16)
        grouped = dot(jnp.concatenate([top, mid, low], axis=0), member[...])
        grouped = ((grouped[8:12] + grouped[4:8]) + grouped[0:4]) * (1.0 / COUNT)
        centre = grouped[0:2]
        variance = grouped[2:4] - centre * centre
        scale = lax.rsqrt(variance + EPS) * gain[...].reshape(1, C)
        return scale, -centre * scale

    def exchange_drain(phase):
        def drain(i, carry):
            stat_copy(phase, lax.rem(tile + i, TILES), tile).wait_send()
            return carry

        lax.fori_loop(1, TILES, drain, 0)
        for copy in halo_copies(phase):
            copy.wait_send()

    def put_taps(f, start, rows, value, scale, shift, keep=None):
        a = silu(value.astype(F32) * scale + shift)
        if keep is not None:
            a = jnp.where(keep, a, 0.0)
        column = lax.broadcasted_iota(jnp.int32, (rows * W, C), 0) & (W - 1)
        before = jnp.where(column == 0, 0.0, pltpu.roll(a, 1, 0))
        after = jnp.where(column == W - 1, 0.0, pltpu.roll(a, rows * W - 1, 0))
        taps[f, pl.ds(start, rows * W), :] = jnp.concatenate(
            [before.astype(BF16), a.astype(BF16), after.astype(BF16)], axis=1
        )

    def fill_own(source, scale, shift):
        for f in range(2):
            put_taps(f, W, ROWS, source[f], scale[f : f + 1], shift[f : f + 1])

    def fill_edges(phase, scale, shift):
        for way, (start, keep) in enumerate(((0, tile > 0), ((ROWS + 1) * W, tile < TILES - 1))):
            for f in range(2):
                value = jnp.concatenate(
                    [
                        halo[phase, way, 2 * f],
                        halo[phase, way, 2 * f + 1],
                        halo[phase, way, 4][:, f * 64 : (f + 1) * 64],
                    ],
                    axis=1,
                )
                put_taps(f, start, 1, value, scale[f : f + 1], shift[f : f + 1], keep)

    def convolve(chunk, weights):
        total = None
        for a in range(3):
            lines = [
                taps[f, pl.ds((row + a) * W, W), :] for row in CHUNKS[chunk] for f in range(2)
            ]
            term = dot(jnp.concatenate(lines, axis=0), weights[a])
            total = term if total is None else total + term
        return total

    def first_convolution(chunk):
        value = convolve(chunk, w_one).astype(BF16)
        sums = []
        for q, row in enumerate(CHUNKS[chunk]):
            for f in range(2):
                hid[f, pl.ds(row * W, W), :] = value[(2 * q + f) * W : (2 * q + f + 1) * W]
        wide = value.astype(F32)
        for f in range(2):
            parts = [wide[(2 * q + f) * W : (2 * q + f + 1) * W] for q in range(len(CHUNKS[chunk]))]
            sums.append(jnp.concatenate(parts, axis=0))
        return channel_sums(sums)

    stats_start(0)
    halo_start(0)
    scale, shift = stats_finish(0, first, gain_one)
    fill_own(lat, scale, shift)
    loads[1].wait()
    second = first_convolution(0)
    halo_finish(0)
    fill_edges(0, scale, shift)
    second = second + first_convolution(1)
    stat_send[1] = second
    pack_halo(1, hid)

    stats_start(1)
    halo_start(1)
    exchange_drain(0)
    loads[2].wait()
    scale, shift = stats_finish(1, second, gain_two)
    fill_own(hid, scale, shift)

    def a2a_copy(way, chunk, source, target, peer, slot):
        return pltpu.make_async_remote_copy(
            src_ref=source.at[peer],
            dst_ref=target.at[slot],
            send_sem=a2a_send_sem.at[way, chunk, peer],
            recv_sem=a2a_recv_sem.at[way, chunk, slot],
            device_id={"clip": peer},
            device_id_type=MESH,
        )

    def pack_row(r, value):
        base = r * 10 * CLIPS
        packed[pl.ds(base, 128), :] = value[:, 0:128]
        packed[pl.ds(base + 128, 128), :] = value[:, 128:256]
        packed[pl.ds(base + 256, 64), :] = jnp.concatenate(
            [value[0:64, 256:320], value[64:128, 256:320]], axis=1
        )

    def peer_at(i, sign):
        block, place = lax.div(i, 8), lax.rem(i, 8)
        mixed = lax.rem(i, 2)
        outer = jnp.logical_or(block == 0, block == 3)
        rest = jnp.where(outer, place, lax.div(i - 8, 2))
        step_z = jnp.where(block == 0, 2, jnp.where(block == 3, 0, 1 + 2 * mixed))
        turn = lax.div(rest, 2)
        step_x = jnp.where(turn == 3, 0, jnp.where(turn == 2, 3, 2 - turn))
        flip = 1 - lax.rem(rest, 2)
        x, z, core = lax.div(clip, 8), lax.rem(lax.div(clip, 2), 4), lax.rem(clip, 2)
        x = lax.rem(x + sign * step_x + 4, 4)
        z = lax.rem(z + sign * step_z + 4, 4)
        return (x * 4 + z) * 2 + lax.rem(core + flip, 2)

    def a2a_start(way, chunk, source, target):
        depth = len(CHUNKS[chunk]) * 10

        def pick(peer):
            base = STARTS[chunk] * 10 * CLIPS
            return packed[pl.ds(base + peer, depth, stride=CLIPS), :].astype(BF16)

        def stage(i, carry):
            peer = peer_at(i, 1)
            source[peer] = pick(peer)
            return carry

        def send(i, carry):
            peer = peer_at(i, 1)
            a2a_copy(way, chunk, source, target, peer, clip).start()
            return carry

        lax.fori_loop(0, 8, stage, 0)
        for block in range(3):
            lax.fori_loop(block * 8 + 8, min(block * 8 + 16, 31), stage, 0)
            lax.fori_loop(block * 8, block * 8 + 8, send, 0)
        target[clip] = pick(clip)
        lax.fori_loop(24, 31, send, 0)

    def a2a_finish(way, chunk, source, target):
        depth = len(CHUNKS[chunk]) * 10

        def widen(peer):
            spread[pl.ds(pl.multiple_of(peer * 32, 32), depth), :] = target[peer].astype(F32)

        def arrive(i, carry):
            peer = peer_at(i, -1)
            a2a_copy(way, chunk, source, target, peer, peer).wait_recv()
            widen(peer)
            return carry

        widen(clip)
        lax.fori_loop(0, 31, arrive, 0)
        return [unpack_row(q) for q in range(len(CHUNKS[chunk]))]

    def a2a_drain(way, chunk, source, target):
        def drain(i, carry):
            peer = peer_at(i, 1)
            a2a_copy(way, chunk, source, target, peer, clip).wait_send()
            return carry

        lax.fori_loop(0, 31, drain, 0)

    def unpack_row(q):
        def column(k):
            return spread[pl.ds(q * 10 + k, CLIPS, stride=32), :]

        left = jnp.concatenate([column(k) for k in range(4)], axis=0)
        middle = jnp.concatenate([column(4 + k) for k in range(4)], axis=0)
        tail = jnp.concatenate([column(8), column(9)], axis=0)
        right = jnp.concatenate([tail, pltpu.roll(tail, 64, 1)], axis=0)
        return jnp.concatenate([left, middle, right[:, 0:64]], axis=1)

    one_live = length[0] == 1
    sends, recvs = (send_0, send_1), (recv_0, recv_1)
    back_sends, back_recvs = (back_send_0, back_send_1), (back_recv_0, back_recv_1)

    for chunk in range(2):
        if chunk == 1:
            halo_finish(1)
            fill_edges(1, scale, shift)
        total = convolve(chunk, w_two)
        for q, row in enumerate(CHUNKS[chunk]):
            halves = []
            for f in range(2):
                span = slice((2 * q + f) * W, (2 * q + f + 1) * W)
                value = lat[f, pl.ds(row * W, W), :].astype(F32) + total[span]
                halves.append(jnp.where(one_live, DEAD, value) if f == 1 else value)
            pack_row(STARTS[chunk] + q, jnp.concatenate(halves, axis=0))
        a2a_start(0, chunk, sends[chunk], recvs[chunk])

    for load in loads[3:]:
        load.wait()
    exchange_drain(1)

    lane = lax.broadcasted_iota(jnp.int32, (128, 128), 1)
    line = lax.broadcasted_iota(jnp.int32, (128, 128), 0)
    lane_clip, lane_cell, lane_slot = lane & 31, (lane >> 5) & 1, lane >> 6
    line_clip, line_cell = line & 31, (line >> 5) & 1
    lane_frame = lane_clip * 2 + lane_slot
    shared = jnp.zeros((128, 128), F32)
    for j in range(8):
        shared = shared + jnp.where(lane_frame == context[j], 1.0, 0.0)
    low_half = lane < HEAD_DIM
    clip_row = lax.broadcasted_iota(jnp.int32, (CLIPS, C), 0)

    for chunk in range(2):
        rows = len(CHUNKS[chunk])
        blocks = a2a_finish(0, chunk, sends[chunk], recvs[chunk])
        dead = jnp.broadcast_to(blocks[0][64:96, 0:1], (CLIPS, 128)) > DEAD_LIMIT
        dead_wide = jnp.broadcast_to(blocks[0][64:96, 0:1], (CLIPS, C)) > DEAD_LIMIT
        dead_f = jnp.where(dead, 1.0, 0.0)
        dead_lane = jnp.sum(
            jnp.where(
                lax.broadcasted_iota(jnp.int32, (CLIPS, 128), 0)
                == (lax.broadcasted_iota(jnp.int32, (CLIPS, 128), 1) & 31),
                dead_f,
                0.0,
            ),
            axis=0,
            keepdims=True,
        )
        live_key = 1.0 - jnp.where(lane_slot == 1, jnp.broadcast_to(dead_lane, (128, 128)), 0.0)
        weight = jnp.where(
            lane_cell == line_cell,
            jnp.where(lane_clip == line_clip, live_key, 0.0) + shared,
            0.0,
        )
        visible = weight > 0.0
        weight2 = jnp.concatenate([weight, weight], axis=1)
        visible2 = jnp.concatenate([visible, visible], axis=1)

        sources = []
        for q in range(rows):
            x = jnp.where(blocks[q] > DEAD_LIMIT, 0.0, blocks[q])
            sources.append(x)
            moving = rounded(silu(x))
            before, after = [None] * 4, [None] * 4
            for cell in range(2):
                m0 = moving[cell * 32 : cell * 32 + 32]
                m1 = moving[64 + cell * 32 : 96 + cell * 32]
                final = jnp.where(dead_wide, m0, m1)
                prior = jnp.where(clip_row == 0, 0.0, pltpu.roll(final, 1, 0))
                later = jnp.where(clip_row == CLIPS - 1, 0.0, pltpu.roll(m0, CLIPS - 1, 0))
                before[cell], before[2 + cell] = prior, m0
                after[cell], after[2 + cell] = jnp.where(dead_wide, later, m1), later
            taps[0, pl.ds(q * 128, 128), :] = jnp.concatenate(
                [
                    jnp.concatenate(before, axis=0).astype(BF16),
                    moving.astype(BF16),
                    jnp.concatenate(after, axis=0).astype(BF16),
                ],
                axis=1,
            )
        source = jnp.concatenate(sources, axis=0)
        res_two = rounded(source + dot(taps[0, pl.ds(0, rows * 128), :], w_time[...]))
        centre = jnp.mean(res_two, axis=1, keepdims=True)
        offset = res_two - centre
        variance = jnp.mean(offset * offset, axis=1, keepdims=True)
        normed = (offset * lax.rsqrt(variance + EPS) * gain_attn[...].reshape(1, C)).astype(BF16)
        q_all = dot(normed, w_qkv[:, 0:C]).astype(BF16)
        k_all = dot(normed, w_qkv[:, C : 2 * C]).astype(BF16)
        v_all = dot(normed, w_qkv[:, 2 * C : 3 * C]).astype(BF16)
        zero = jnp.zeros((128, 128), BF16)
        attended = []
        for q in range(rows):
            span = slice(q * 128, (q + 1) * 128)
            pieces = []
            for pair in range(2):
                cols = slice(pair * 128, (pair + 1) * 128)
                queries, keys, values = q_all[span, cols], k_all[span, cols], v_all[span, cols]
                keys2 = jnp.concatenate(
                    [jnp.where(low_half, keys, zero), jnp.where(low_half, zero, keys)], axis=0
                )
                values2 = jnp.concatenate(
                    [jnp.where(low_half, values, zero), jnp.where(low_half, zero, values)], axis=0
                )
                scores = lax.dot_general(
                    queries, keys2, (((1,), (1,)), ((), ())), preferred_element_type=F32
                ) * (HEAD_DIM**-0.5)
                scores = jnp.where(visible2, scores, MASKED)
                top = jnp.concatenate(
                    [
                        jnp.broadcast_to(
                            jnp.max(scores[:, i * 128 : (i + 1) * 128], axis=1, keepdims=True),
                            (128, 128),
                        )
                        for i in range(2)
                    ],
                    axis=1,
                )
                grown = jnp.exp(scores - top) * weight2
                norm = jnp.where(
                    low_half,
                    jnp.broadcast_to(jnp.sum(grown[:, 0:128], axis=1, keepdims=True), (128, 128)),
                    jnp.broadcast_to(jnp.sum(grown[:, 128:256], axis=1, keepdims=True), (128, 128)),
                )
                pieces.append((dot(grown.astype(BF16), values2) / norm).astype(BF16))
            cols = slice(256, 320)
            scores = lax.dot_general(
                q_all[span, cols], k_all[span, cols], (((1,), (1,)), ((), ())),
                preferred_element_type=F32,
            ) * (HEAD_DIM**-0.5)
            scores = jnp.where(visible, scores, MASKED)
            grown = jnp.exp(scores - jnp.max(scores, axis=1, keepdims=True)) * weight
            norm = jnp.sum(grown, axis=1, keepdims=True)
            pieces.append((dot(grown.astype(BF16), v_all[span, cols]) / norm).astype(BF16))
            attended.append(jnp.concatenate(pieces, axis=1))
        result = res_two + dot(jnp.concatenate(attended, axis=0), w_out[...])
        for q in range(rows):
            block = result[q * 128 : (q + 1) * 128]
            parts = [block[0:64]]
            for cell in range(2):
                parts.append(jnp.where(dead_wide, 0.0, block[64 + cell * 32 : 96 + cell * 32]))
            pack_row(STARTS[chunk] + q, jnp.concatenate(parts, axis=0))
        a2a_start(1, chunk, back_sends[chunk], back_recvs[chunk])

    for chunk in range(2):
        a2a_drain(0, chunk, sends[chunk], recvs[chunk])
    for chunk in range(2):
        blocks = a2a_finish(1, chunk, back_sends[chunk], back_recvs[chunk])
        for q, row in enumerate(CHUNKS[chunk]):
            for f in range(2):
                out[f, pl.ds(row * W, W), :] = blocks[q][f * 64 : (f + 1) * 64].astype(BF16)
    for chunk in range(2):
        a2a_drain(1, chunk, back_sends[chunk], back_recvs[chunk])


def local(
    latents, lengths, context, gain_first, conv_first, gain_second, conv_second,
    time_weight, attn_gain, w_qkv, w_out,
):
    vmem = pl.BlockSpec(memory_space=pltpu.VMEM)
    smem = pl.BlockSpec(memory_space=pltpu.SMEM)
    hbm = pl.BlockSpec(memory_space=pl.ANY)

    def messages(chunk):
        return pltpu.VMEM((CLIPS, len(CHUNKS[chunk]) * 10, 128), BF16)

    result = pl.pallas_call(
        kernel,
        out_shape=jax.ShapeDtypeStruct((2, ROWS * W, C), BF16),
        in_specs=[hbm, smem, smem, vmem, vmem, vmem, hbm, hbm, hbm, hbm, hbm],
        out_specs=vmem,
        scratch_shapes=[
            pltpu.VMEM((2, ROWS * W, C), BF16),
            pltpu.VMEM((3, 3 * C, C), BF16),
            pltpu.VMEM((3, 3 * C, C), BF16),
            pltpu.VMEM((3 * C, C), BF16),
            pltpu.VMEM((C, 3 * C), BF16),
            pltpu.VMEM((C, C), BF16),
            pltpu.VMEM((2, (ROWS + 2) * W, 3 * C), BF16),
            pltpu.VMEM((2, ROWS * W, C), BF16),
            pltpu.VMEM((2, 2, 5, W, 128), BF16),
            pltpu.VMEM((2, 2, 5, W, 128), BF16),
            pltpu.VMEM((C, C), BF16),
            pltpu.VMEM((2, 4, C), F32),
            pltpu.VMEM((2, TILES, 4, C), F32),
            pltpu.VMEM((ROWS * 10 * CLIPS, 128), F32),
            pltpu.VMEM((CLIPS * 32, 128), F32),
            messages(0), messages(1), messages(0), messages(1),
            messages(0), messages(1), messages(0), messages(1),
            pltpu.SemaphoreType.DMA((6,)),
            pltpu.SemaphoreType.DMA((2, 2)),
            pltpu.SemaphoreType.DMA((2, 2)),
            pltpu.SemaphoreType.DMA((2, TILES)),
            pltpu.SemaphoreType.DMA((2, TILES)),
            pltpu.SemaphoreType.DMA((2, 2, CLIPS)),
            pltpu.SemaphoreType.DMA((2, 2, CLIPS)),
        ],
        compiler_params=pltpu.CompilerParams(
            collective_id=0, has_side_effects=True, vmem_limit_bytes=67043328
        ),
        name="block",
    )(
        latents.reshape(2, ROWS * W, C),
        lengths,
        context,
        gain_first,
        gain_second,
        attn_gain,
        conv_first.reshape(3, 3 * C, C),
        conv_second.reshape(3, 3 * C, C),
        time_weight.reshape(3 * C, C),
        w_qkv,
        w_out,
    )
    return result.reshape(2, ROWS, W, C)


def solution(mesh):
    placed = (P("clip", "tile", None, None), P("clip"), P(), P(), P(), P(), P(), P(), P(), P(), P())
    return jax.shard_map(
        local, mesh=mesh, in_specs=placed, out_specs=P("clip", "tile", None, None), check_vma=False
    )
```

```python
import jax
import jax.numpy as jnp
from jax import lax
from jax.experimental import pallas as pl
from jax.experimental.pallas import tpu as pltpu
from jax.sharding import PartitionSpec as P

MESH = pl.DeviceIdType.MESH
F32 = jnp.float32
BF16 = jnp.bfloat16

C = 320
HEAD_DIM = 64
HEADS = 5
GROUP_WIDTH = 10
H = 40
W = 64
ROWS = 5
CLIPS = 32
TILES = 8
COUNT = H * W * GROUP_WIDTH
EPS = 1e-05
MASKED = -1e30
DEAD = 1e30
DEAD_LIMIT = 1e20
CHUNKS = ((1, 2, 3), (0, 4))
STARTS = (0, 3)


def wrap(value, size):
    return jnp.where(value >= size, value - size, value)


def dot(a, b):
    return jnp.dot(a, b, preferred_element_type=F32)


def silu(y):
    half = 0.5 * y
    return half + half * jnp.tanh(half)


def rounded(v):
    return v.astype(BF16).astype(F32)


def channel_sums(frames):
    sums = [jnp.sum(v, axis=0, keepdims=True) for v in frames]
    squares = [jnp.sum(v * v, axis=0, keepdims=True) for v in frames]
    return jnp.concatenate(sums + squares, axis=0)


def kernel(
    lat_hbm, length_hbm, context_hbm, gain_one_hbm, gain_two_hbm, gain_attn_hbm,
    w_one_hbm, w_two_hbm, w_time_hbm, w_qkv_hbm, w_out_hbm,
    out,
    lat, length, context, gain_one, gain_two, gain_attn, w_one, w_two, w_time, w_qkv, w_out,
    taps, hid, halo_send, halo, member, stat_send, stat_recv, packed, spread,
    send_0, send_1, recv_0, recv_1, back_send_0, back_send_1, back_recv_0, back_recv_1,
    load_sem, halo_send_sem, halo_recv_sem, stat_send_sem, stat_recv_sem,
    a2a_send_sem, a2a_recv_sem,
):
    clip = lax.axis_index("clip")
    tile = lax.axis_index("tile")
    tile_up, tile_down = wrap(tile + TILES - 1, TILES), wrap(tile + 1, TILES)

    loads = [
        pltpu.make_async_copy(source, target, load_sem.at[i])
        for i, (source, target) in enumerate(
            (
                (lat_hbm, lat),
                (length_hbm, length),
                (context_hbm, context),
                (gain_one_hbm, gain_one),
                (gain_two_hbm, gain_two),
                (gain_attn_hbm, gain_attn),
                (w_one_hbm, w_one),
                (w_two_hbm, w_two),
                (w_time_hbm, w_time),
                (w_qkv_hbm, w_qkv),
                (w_out_hbm, w_out),
            )
        )
    ]
    for load in loads:
        load.start()

    barrier = pltpu.get_barrier_semaphore()

    for i in range(1, CLIPS):
        pl.semaphore_signal(
            barrier, inc=1, device_id={"clip": wrap(clip + i, CLIPS)}, device_id_type=MESH
        )
    for i in range(1, TILES):
        pl.semaphore_signal(
            barrier, inc=1, device_id={"tile": wrap(tile + i, TILES)}, device_id_type=MESH
        )

    rows = lax.broadcasted_iota(jnp.int32, (C, C), 0)
    cols = lax.broadcasted_iota(jnp.int32, (C, C), 1)
    member[...] = jnp.where(((rows * 6554) >> 16) == ((cols * 6554) >> 16), 1.0, 0.0).astype(BF16)

    def pack_halo(phase, source):
        for way, start in enumerate(((ROWS - 1) * W, 0)):
            span = pl.ds(start, W)
            for f in range(2):
                halo_send[phase, way, 2 * f] = source[f, span, 0:128]
                halo_send[phase, way, 2 * f + 1] = source[f, span, 128:256]
            halo_send[phase, way, 4] = jnp.concatenate(
                [source[0, span, 256:320], source[1, span, 256:320]], axis=1
            )

    for load in loads[:6]:
        load.wait()
    pack_halo(0, lat)
    first = channel_sums([lat[0].astype(F32), lat[1].astype(F32)])
    stat_send[0] = first
    pl.semaphore_wait(barrier, TILES - 1 + CLIPS - 1)

    def halo_copies(phase):
        return [
            pltpu.make_async_remote_copy(
                src_ref=halo_send.at[phase, way],
                dst_ref=halo.at[phase, way],
                send_sem=halo_send_sem.at[phase, way],
                recv_sem=halo_recv_sem.at[phase, way],
                device_id={"tile": peer},
                device_id_type=MESH,
            )
            for way, peer in enumerate((tile_down, tile_up))
        ]

    def stats_start(phase):
        for i in range(1, TILES):
            pltpu.make_async_remote_copy(
                src_ref=stat_send.at[phase],
                dst_ref=stat_recv.at[phase, tile],
                send_sem=stat_send_sem.at[phase],
                recv_sem=stat_recv_sem.at[phase],
                device_id={"tile": wrap(tile + i, TILES)},
                device_id_type=MESH,
            ).start()

    def batch_wait(buffer, count, sem):
        span = buffer.at[pl.ds(0, count)]
        pltpu.make_async_copy(span, span, sem).wait()

    def halo_start(phase):
        for copy in halo_copies(phase):
            copy.start()

    def halo_finish(phase):
        for copy in halo_copies(phase):
            copy.wait_recv()

    def stats_finish(phase, own, gain):
        stat_recv[phase, tile] = own

        batch_wait(stat_recv.at[phase], TILES - 1, stat_recv_sem.at[phase])
        total = stat_recv[phase, 0]
        for i in range(1, TILES):
            total = total + stat_recv[phase, i]
        top = total.astype(BF16)
        rest = total - top.astype(F32)
        mid = rest.astype(BF16)
        low = (rest - mid.astype(F32)).astype(BF16)
        grouped = dot(jnp.concatenate([top, mid, low], axis=0), member[...])
        grouped = ((grouped[8:12] + grouped[4:8]) + grouped[0:4]) * (1.0 / COUNT)
        centre = grouped[0:2]
        variance = grouped[2:4] - centre * centre
        scale = lax.rsqrt(variance + EPS) * gain[...].reshape(1, C)
        return scale, -centre * scale

    def exchange_drain(phase):
        batch_wait(stat_recv.at[phase], TILES - 1, stat_send_sem.at[phase])
        for copy in halo_copies(phase):
            copy.wait_send()

    def put_taps(f, start, rows, value, scale, shift, keep=None):
        a = silu(value.astype(F32) * scale + shift)
        if keep is not None:
            a = jnp.where(keep, a, 0.0)
        column = lax.broadcasted_iota(jnp.int32, (rows * W, C), 0) & (W - 1)
        before = jnp.where(column == 0, 0.0, pltpu.roll(a, 1, 0))
        after = jnp.where(column == W - 1, 0.0, pltpu.roll(a, rows * W - 1, 0))
        taps[f, pl.ds(start, rows * W), :] = jnp.concatenate(
            [before.astype(BF16), a.astype(BF16), after.astype(BF16)], axis=1
        )

    def fill_own(source, scale, shift):
        for f in range(2):
            put_taps(f, W, ROWS, source[f], scale[f : f + 1], shift[f : f + 1])

    def fill_edges(phase, scale, shift):
        for way, (start, keep) in enumerate(((0, tile > 0), ((ROWS + 1) * W, tile < TILES - 1))):
            for f in range(2):
                value = jnp.concatenate(
                    [
                        halo[phase, way, 2 * f],
                        halo[phase, way, 2 * f + 1],
                        halo[phase, way, 4][:, f * 64 : (f + 1) * 64],
                    ],
                    axis=1,
                )
                put_taps(f, start, 1, value, scale[f : f + 1], shift[f : f + 1], keep)

    def convolve(chunk, weights):
        total = None
        for a in range(3):
            lines = [
                taps[f, pl.ds((row + a) * W, W), :] for row in CHUNKS[chunk] for f in range(2)
            ]
            term = dot(jnp.concatenate(lines, axis=0), weights[a])
            total = term if total is None else total + term
        return total

    def first_convolution(chunk):
        value = convolve(chunk, w_one).astype(BF16)
        sums = []
        for q, row in enumerate(CHUNKS[chunk]):
            for f in range(2):
                hid[f, pl.ds(row * W, W), :] = value[(2 * q + f) * W : (2 * q + f + 1) * W]
        wide = value.astype(F32)
        for f in range(2):
            parts = [wide[(2 * q + f) * W : (2 * q + f + 1) * W] for q in range(len(CHUNKS[chunk]))]
            sums.append(jnp.concatenate(parts, axis=0))
        return channel_sums(sums)

    stats_start(0)
    halo_start(0)
    scale, shift = stats_finish(0, first, gain_one)
    fill_own(lat, scale, shift)
    loads[6].wait()
    second = first_convolution(0)
    halo_finish(0)
    fill_edges(0, scale, shift)
    second = second + first_convolution(1)
    stat_send[1] = second
    pack_halo(1, hid)

    stats_start(1)
    halo_start(1)
    exchange_drain(0)
    loads[7].wait()
    scale, shift = stats_finish(1, second, gain_two)
    fill_own(hid, scale, shift)

    def pack_row(r, value):
        base = r * 10 * CLIPS
        packed[pl.ds(base, 128), :] = value[:, 0:128]
        packed[pl.ds(base + 128, 128), :] = value[:, 128:256]
        packed[pl.ds(base + 256, 64), :] = jnp.concatenate(
            [value[0:64, 256:320], value[64:128, 256:320]], axis=1
        )

    def a2a_start(way, chunk, source, target):
        depth = len(CHUNKS[chunk]) * 10
        base = STARTS[chunk] * 10 * CLIPS
        for peer in range(CLIPS):
            source[peer] = packed[pl.ds(base + peer, depth, stride=CLIPS), :].astype(BF16)
        target[clip] = source[clip]
        for i in range(1, CLIPS):
            peer = wrap(clip + i, CLIPS)
            pltpu.make_async_remote_copy(
                src_ref=source.at[peer],
                dst_ref=target.at[clip],
                send_sem=a2a_send_sem.at[way, chunk],
                recv_sem=a2a_recv_sem.at[way, chunk],
                device_id={"clip": peer},
                device_id_type=MESH,
            ).start()

    def a2a_finish(way, chunk, source, target):
        depth = len(CHUNKS[chunk]) * 10
        batch_wait(target, CLIPS - 1, a2a_recv_sem.at[way, chunk])
        for peer in range(CLIPS):
            spread[pl.ds(peer * 32, depth), :] = target[peer].astype(F32)
        return [unpack_row(q) for q in range(len(CHUNKS[chunk]))]

    def a2a_drain(way, chunk, source, target):
        batch_wait(source, CLIPS - 1, a2a_send_sem.at[way, chunk])

    def unpack_row(q):
        def column(k):
            return spread[pl.ds(q * 10 + k, CLIPS, stride=32), :]

        left = jnp.concatenate([column(k) for k in range(4)], axis=0)
        middle = jnp.concatenate([column(4 + k) for k in range(4)], axis=0)
        tail = jnp.concatenate([column(8), column(9)], axis=0)
        right = jnp.concatenate([tail, pltpu.roll(tail, 64, 1)], axis=0)
        return jnp.concatenate([left, middle, right[:, 0:64]], axis=1)

    one_live = length[0] == 1
    sends, recvs = (send_0, send_1), (recv_0, recv_1)
    back_sends, back_recvs = (back_send_0, back_send_1), (back_recv_0, back_recv_1)

    for chunk in range(2):
        if chunk == 1:
            halo_finish(1)
            fill_edges(1, scale, shift)
        total = convolve(chunk, w_two)
        for q, row in enumerate(CHUNKS[chunk]):
            halves = []
            for f in range(2):
                span = slice((2 * q + f) * W, (2 * q + f + 1) * W)
                value = lat[f, pl.ds(row * W, W), :].astype(F32) + total[span]
                halves.append(jnp.where(one_live, DEAD, value) if f == 1 else value)
            pack_row(STARTS[chunk] + q, jnp.concatenate(halves, axis=0))
        a2a_start(0, chunk, sends[chunk], recvs[chunk])

    for load in loads[8:]:
        load.wait()
    exchange_drain(1)

    lane = lax.broadcasted_iota(jnp.int32, (128, 128), 1)
    line = lax.broadcasted_iota(jnp.int32, (128, 128), 0)
    lane_clip, lane_cell, lane_slot = lane & 31, (lane >> 5) & 1, lane >> 6
    line_clip, line_cell = line & 31, (line >> 5) & 1
    lane_frame = lane_clip * 2 + lane_slot
    shared = jnp.zeros((128, 128), F32)
    for j in range(8):
        shared = shared + jnp.where(lane_frame == context[j], 1.0, 0.0)
    low_half = lane < HEAD_DIM
    clip_row = lax.broadcasted_iota(jnp.int32, (CLIPS, C), 0)

    for chunk in range(2):
        rows = len(CHUNKS[chunk])
        blocks = a2a_finish(0, chunk, sends[chunk], recvs[chunk])
        dead = jnp.broadcast_to(blocks[0][64:96, 0:1], (CLIPS, 128)) > DEAD_LIMIT
        dead_wide = jnp.broadcast_to(blocks[0][64:96, 0:1], (CLIPS, C)) > DEAD_LIMIT
        dead_f = jnp.where(dead, 1.0, 0.0)
        dead_lane = jnp.sum(
            jnp.where(
                lax.broadcasted_iota(jnp.int32, (CLIPS, 128), 0)
                == (lax.broadcasted_iota(jnp.int32, (CLIPS, 128), 1) & 31),
                dead_f,
                0.0,
            ),
            axis=0,
            keepdims=True,
        )
        live_key = 1.0 - jnp.where(lane_slot == 1, jnp.broadcast_to(dead_lane, (128, 128)), 0.0)
        weight = jnp.where(
            lane_cell == line_cell,
            jnp.where(lane_clip == line_clip, live_key, 0.0) + shared,
            0.0,
        )
        visible = weight > 0.0
        weight2 = jnp.concatenate([weight, weight], axis=1)
        visible2 = jnp.concatenate([visible, visible], axis=1)

        sources = []
        for q in range(rows):
            x = jnp.where(blocks[q] > DEAD_LIMIT, 0.0, blocks[q])
            sources.append(x)
            moving = rounded(silu(x))
            before, after = [None] * 4, [None] * 4
            for cell in range(2):
                m0 = moving[cell * 32 : cell * 32 + 32]
                m1 = moving[64 + cell * 32 : 96 + cell * 32]
                final = jnp.where(dead_wide, m0, m1)
                prior = jnp.where(clip_row == 0, 0.0, pltpu.roll(final, 1, 0))
                later = jnp.where(clip_row == CLIPS - 1, 0.0, pltpu.roll(m0, CLIPS - 1, 0))
                before[cell], before[2 + cell] = prior, m0
                after[cell], after[2 + cell] = jnp.where(dead_wide, later, m1), later
            taps[0, pl.ds(q * 128, 128), :] = jnp.concatenate(
                [
                    jnp.concatenate(before, axis=0).astype(BF16),
                    moving.astype(BF16),
                    jnp.concatenate(after, axis=0).astype(BF16),
                ],
                axis=1,
            )
        source = jnp.concatenate(sources, axis=0)
        res_two = rounded(source + dot(taps[0, pl.ds(0, rows * 128), :], w_time[...]))
        centre = jnp.mean(res_two, axis=1, keepdims=True)
        offset = res_two - centre
        variance = jnp.mean(offset * offset, axis=1, keepdims=True)
        normed = (offset * lax.rsqrt(variance + EPS) * gain_attn[...].reshape(1, C)).astype(BF16)
        q_all = dot(normed, w_qkv[:, 0:C]).astype(BF16)
        k_all = dot(normed, w_qkv[:, C : 2 * C]).astype(BF16)
        v_all = dot(normed, w_qkv[:, 2 * C : 3 * C]).astype(BF16)
        zero = jnp.zeros((128, 128), BF16)
        attended = []
        for q in range(rows):
            span = slice(q * 128, (q + 1) * 128)
            pieces = []
            for pair in range(2):
                cols = slice(pair * 128, (pair + 1) * 128)
                queries, keys, values = q_all[span, cols], k_all[span, cols], v_all[span, cols]
                keys2 = jnp.concatenate(
                    [jnp.where(low_half, keys, zero), jnp.where(low_half, zero, keys)], axis=0
                )
                values2 = jnp.concatenate(
                    [jnp.where(low_half, values, zero), jnp.where(low_half, zero, values)], axis=0
                )
                scores = lax.dot_general(
                    queries, keys2, (((1,), (1,)), ((), ())), preferred_element_type=F32
                ) * (HEAD_DIM**-0.5)
                scores = jnp.where(visible2, scores, MASKED)
                top = jnp.concatenate(
                    [
                        jnp.broadcast_to(
                            jnp.max(scores[:, i * 128 : (i + 1) * 128], axis=1, keepdims=True),
                            (128, 128),
                        )
                        for i in range(2)
                    ],
                    axis=1,
                )
                grown = jnp.exp(scores - top) * weight2
                norm = jnp.where(
                    low_half,
                    jnp.broadcast_to(jnp.sum(grown[:, 0:128], axis=1, keepdims=True), (128, 128)),
                    jnp.broadcast_to(jnp.sum(grown[:, 128:256], axis=1, keepdims=True), (128, 128)),
                )
                pieces.append((dot(grown.astype(BF16), values2) / norm).astype(BF16))
            cols = slice(256, 320)
            scores = lax.dot_general(
                q_all[span, cols], k_all[span, cols], (((1,), (1,)), ((), ())),
                preferred_element_type=F32,
            ) * (HEAD_DIM**-0.5)
            scores = jnp.where(visible, scores, MASKED)
            grown = jnp.exp(scores - jnp.max(scores, axis=1, keepdims=True)) * weight
            norm = jnp.sum(grown, axis=1, keepdims=True)
            pieces.append((dot(grown.astype(BF16), v_all[span, cols]) / norm).astype(BF16))
            attended.append(jnp.concatenate(pieces, axis=1))
        result = res_two + dot(jnp.concatenate(attended, axis=0), w_out[...])
        for q in range(rows):
            block = result[q * 128 : (q + 1) * 128]
            parts = [block[0:64]]
            for cell in range(2):
                parts.append(jnp.where(dead_wide, 0.0, block[64 + cell * 32 : 96 + cell * 32]))
            pack_row(STARTS[chunk] + q, jnp.concatenate(parts, axis=0))
        a2a_start(1, chunk, back_sends[chunk], back_recvs[chunk])

    for chunk in range(2):
        a2a_drain(0, chunk, sends[chunk], recvs[chunk])
    for chunk in range(2):
        blocks = a2a_finish(1, chunk, back_sends[chunk], back_recvs[chunk])
        for q, row in enumerate(CHUNKS[chunk]):
            for f in range(2):
                out[f, pl.ds(row * W, W), :] = blocks[q][f * 64 : (f + 1) * 64].astype(BF16)
    for chunk in range(2):
        a2a_drain(1, chunk, back_sends[chunk], back_recvs[chunk])


def local(
    latents, lengths, context, gain_first, conv_first, gain_second, conv_second,
    time_weight, attn_gain, w_qkv, w_out,
):
    vmem = pl.BlockSpec(memory_space=pltpu.VMEM)
    hbm = pl.BlockSpec(memory_space=pltpu.HBM)

    def messages(chunk):
        return pltpu.VMEM((CLIPS, len(CHUNKS[chunk]) * 10, 128), BF16)

    result = pl.pallas_call(
        kernel,
        out_shape=jax.ShapeDtypeStruct((2, ROWS * W, C), BF16),
        in_specs=[hbm] * 11,
        out_specs=vmem,
        scratch_shapes=[
            pltpu.VMEM((2, ROWS * W, C), BF16),
            pltpu.SMEM((1,), jnp.int32),
            pltpu.SMEM((8,), jnp.int32),
            pltpu.VMEM((C,), F32),
            pltpu.VMEM((C,), F32),
            pltpu.VMEM((C,), F32),
            pltpu.VMEM((3, 3 * C, C), BF16),
            pltpu.VMEM((3, 3 * C, C), BF16),
            pltpu.VMEM((3 * C, C), BF16),
            pltpu.VMEM((C, 3 * C), BF16),
            pltpu.VMEM((C, C), BF16),
            pltpu.VMEM((2, (ROWS + 2) * W, 3 * C), BF16),
            pltpu.VMEM((2, ROWS * W, C), BF16),
            pltpu.VMEM((2, 2, 5, W, 128), BF16),
            pltpu.VMEM((2, 2, 5, W, 128), BF16),
            pltpu.VMEM((C, C), BF16),
            pltpu.VMEM((2, 4, C), F32),
            pltpu.VMEM((2, TILES, 4, C), F32),
            pltpu.VMEM((ROWS * 10 * CLIPS, 128), F32),
            pltpu.VMEM((CLIPS * 32, 128), F32),
            messages(0), messages(1), messages(0), messages(1),
            messages(0), messages(1), messages(0), messages(1),
            pltpu.SemaphoreType.DMA((11,)),
            pltpu.SemaphoreType.DMA((2, 2)),
            pltpu.SemaphoreType.DMA((2, 2)),
            pltpu.SemaphoreType.DMA((2,)),
            pltpu.SemaphoreType.DMA((2,)),
            pltpu.SemaphoreType.DMA((2, 2)),
            pltpu.SemaphoreType.DMA((2, 2)),
        ],
        compiler_params=pltpu.CompilerParams(
            collective_id=0, has_side_effects=True, vmem_limit_bytes=56 << 20
        ),
        name="block",
    )(
        latents.reshape(2, ROWS * W, C),
        lengths,
        context,
        gain_first,
        gain_second,
        attn_gain,
        conv_first.reshape(3, 3 * C, C),
        conv_second.reshape(3, 3 * C, C),
        time_weight.reshape(3 * C, C),
        w_qkv,
        w_out,
    )
    return result.reshape(2, ROWS, W, C)


def solution(mesh):
    placed = (P("clip", "tile", None, None), P("clip"), P(), P(), P(), P(), P(), P(), P(), P(), P())
    return jax.shard_map(
        local, mesh=mesh, in_specs=placed, out_specs=P("clip", "tile", None, None), check_vma=False
    )
```

```python
import jax
import jax.numpy as jnp
from jax import lax
from jax.experimental import pallas as pl
from jax.experimental.pallas import tpu as pltpu
from jax.sharding import PartitionSpec as P

MESH = pl.DeviceIdType.MESH
F32 = jnp.float32
BF16 = jnp.bfloat16

C = 320
HEAD_DIM = 64
HEADS = 5
GROUP_WIDTH = 10
H = 40
W = 64
ROWS = 5
CLIPS = 32
TILES = 8
COUNT = H * W * GROUP_WIDTH
EPS = 1e-05
MASKED = -1e30
DEAD = 1e30
DEAD_LIMIT = 1e20
CHUNKS = ((1, 2, 3), (0, 4))
STARTS = (0, 3)


def wrap(value, size):
    return jnp.where(value >= size, value - size, value)


def dot(a, b):
    return jnp.dot(a, b, preferred_element_type=F32)


def silu(y):
    half = 0.5 * y
    return half + half * jnp.tanh(half)


def rounded(v):
    return v.astype(BF16).astype(F32)


def channel_sums(frames):
    sums = [jnp.sum(v, axis=0, keepdims=True) for v in frames]
    squares = [jnp.sum(v * v, axis=0, keepdims=True) for v in frames]
    return jnp.concatenate(sums + squares, axis=0)


def kernel(
    lat_hbm, length_hbm, context_hbm, gain_one_hbm, gain_two_hbm, gain_attn_hbm,
    w_one_hbm, w_two_hbm, w_time_hbm, w_qkv_hbm, w_out_hbm,
    out,
    lat, length, context, gain_one, gain_two, gain_attn, w_one, w_two, w_time, w_qkv, w_out,
    taps, hid, halo_send, halo, member, stat_send, stat_recv, packed, spread,
    send_0, send_1, recv_0, recv_1, back_send_0, back_send_1, back_recv_0, back_recv_1,
    load_sem, halo_send_sem, halo_recv_sem, stat_send_sem, stat_recv_sem,
    a2a_send_sem, a2a_recv_sem,
):
    clip = lax.axis_index("clip")
    tile = lax.axis_index("tile")
    tile_up, tile_down = wrap(tile + TILES - 1, TILES), wrap(tile + 1, TILES)

    loads = [
        pltpu.make_async_copy(source, target, load_sem.at[i])
        for i, (source, target) in enumerate(
            (
                (lat_hbm, lat),
                (length_hbm, length),
                (context_hbm, context),
                (gain_one_hbm, gain_one),
                (gain_two_hbm, gain_two),
                (gain_attn_hbm, gain_attn),
                (w_one_hbm, w_one),
                (w_two_hbm, w_two),
                (w_time_hbm, w_time),
                (w_qkv_hbm, w_qkv),
                (w_out_hbm, w_out),
            )
        )
    ]
    for load in loads:
        load.start()

    barrier = pltpu.get_barrier_semaphore()

    for i in range(1, CLIPS):
        pl.semaphore_signal(
            barrier, inc=1, device_id={"clip": wrap(clip + i, CLIPS)}, device_id_type=MESH
        )
    for i in range(1, TILES):
        pl.semaphore_signal(
            barrier, inc=1, device_id={"tile": wrap(tile + i, TILES)}, device_id_type=MESH
        )

    rows = lax.broadcasted_iota(jnp.int32, (C, C), 0)
    cols = lax.broadcasted_iota(jnp.int32, (C, C), 1)
    member[...] = jnp.where(((rows * 6554) >> 16) == ((cols * 6554) >> 16), 1.0, 0.0).astype(BF16)

    def pack_halo(phase, source):
        for way, start in enumerate(((ROWS - 1) * W, 0)):
            span = pl.ds(start, W)
            for f in range(2):
                halo_send[phase, way, 2 * f] = source[f, span, 0:128]
                halo_send[phase, way, 2 * f + 1] = source[f, span, 128:256]
            halo_send[phase, way, 4] = jnp.concatenate(
                [source[0, span, 256:320], source[1, span, 256:320]], axis=1
            )

    for load in loads[:6]:
        load.wait()
    pack_halo(0, lat)
    first = channel_sums([lat[0].astype(F32), lat[1].astype(F32)])
    stat_send[0] = first
    pl.semaphore_wait(barrier, TILES - 1 + CLIPS - 1)

    def halo_copies(phase):
        return [
            pltpu.make_async_remote_copy(
                src_ref=halo_send.at[phase, way],
                dst_ref=halo.at[phase, way],
                send_sem=halo_send_sem.at[phase, way],
                recv_sem=halo_recv_sem.at[phase, way],
                device_id={"tile": peer},
                device_id_type=MESH,
            )
            for way, peer in enumerate((tile_down, tile_up))
        ]

    def stats_start(phase):
        for i in range(1, TILES):
            pltpu.make_async_remote_copy(
                src_ref=stat_send.at[phase],
                dst_ref=stat_recv.at[phase, tile],
                send_sem=stat_send_sem.at[phase],
                recv_sem=stat_recv_sem.at[phase],
                device_id={"tile": wrap(tile + i, TILES)},
                device_id_type=MESH,
            ).start()

    def batch_wait(buffer, count, sem):
        span = buffer.at[pl.ds(0, count)]
        pltpu.make_async_copy(span, span, sem).wait()

    def halo_start(phase):
        for copy in halo_copies(phase):
            copy.start()

    def halo_finish(phase):
        for copy in halo_copies(phase):
            copy.wait_recv()

    def stats_finish(phase, own, gain):
        stat_recv[phase, tile] = own

        batch_wait(stat_recv.at[phase], TILES - 1, stat_recv_sem.at[phase])
        total = stat_recv[phase, 0]
        for i in range(1, TILES):
            total = total + stat_recv[phase, i]
        top = total.astype(BF16)
        rest = total - top.astype(F32)
        mid = rest.astype(BF16)
        low = (rest - mid.astype(F32)).astype(BF16)
        grouped = dot(jnp.concatenate([top, mid, low], axis=0), member[...])
        grouped = ((grouped[8:12] + grouped[4:8]) + grouped[0:4]) * (1.0 / COUNT)
        centre = grouped[0:2]
        variance = grouped[2:4] - centre * centre
        scale = lax.rsqrt(variance + EPS) * gain[...].reshape(1, C)
        return scale, -centre * scale

    def exchange_drain(phase):
        batch_wait(stat_recv.at[phase], TILES - 1, stat_send_sem.at[phase])
        for copy in halo_copies(phase):
            copy.wait_send()

    def put_taps(f, start, rows, value, scale, shift, keep=None):
        a = silu(value.astype(F32) * scale + shift)
        if keep is not None:
            a = jnp.where(keep, a, 0.0)
        column = lax.broadcasted_iota(jnp.int32, (rows * W, C), 0) & (W - 1)
        before = jnp.where(column == 0, 0.0, pltpu.roll(a, 1, 0))
        after = jnp.where(column == W - 1, 0.0, pltpu.roll(a, rows * W - 1, 0))
        taps[f, pl.ds(start, rows * W), :] = jnp.concatenate(
            [before.astype(BF16), a.astype(BF16), after.astype(BF16)], axis=1
        )

    def fill_own(source, scale, shift):
        for f in range(2):
            put_taps(f, W, ROWS, source[f], scale[f : f + 1], shift[f : f + 1])

    def fill_edges(phase, scale, shift):
        for way, (start, keep) in enumerate(((0, tile > 0), ((ROWS + 1) * W, tile < TILES - 1))):
            for f in range(2):
                value = jnp.concatenate(
                    [
                        halo[phase, way, 2 * f],
                        halo[phase, way, 2 * f + 1],
                        halo[phase, way, 4][:, f * 64 : (f + 1) * 64],
                    ],
                    axis=1,
                )
                put_taps(f, start, 1, value, scale[f : f + 1], shift[f : f + 1], keep)

    def convolve(chunk, weights):
        total = None
        for a in range(3):
            lines = [
                taps[f, pl.ds((row + a) * W, W), :] for row in CHUNKS[chunk] for f in range(2)
            ]
            term = dot(jnp.concatenate(lines, axis=0), weights[a])
            total = term if total is None else total + term
        return total

    def first_convolution(chunk):
        value = convolve(chunk, w_one).astype(BF16)
        sums = []
        for q, row in enumerate(CHUNKS[chunk]):
            for f in range(2):
                hid[f, pl.ds(row * W, W), :] = value[(2 * q + f) * W : (2 * q + f + 1) * W]
        wide = value.astype(F32)
        for f in range(2):
            parts = [wide[(2 * q + f) * W : (2 * q + f + 1) * W] for q in range(len(CHUNKS[chunk]))]
            sums.append(jnp.concatenate(parts, axis=0))
        return channel_sums(sums)

    stats_start(0)
    halo_start(0)
    scale, shift = stats_finish(0, first, gain_one)
    fill_own(lat, scale, shift)
    loads[6].wait()
    second = first_convolution(0)
    halo_finish(0)
    fill_edges(0, scale, shift)
    second = second + first_convolution(1)
    stat_send[1] = second
    pack_halo(1, hid)

    stats_start(1)
    halo_start(1)
    exchange_drain(0)
    loads[7].wait()
    scale, shift = stats_finish(1, second, gain_two)
    fill_own(hid, scale, shift)

    def pack_row(r, value):
        base = r * 10 * CLIPS
        packed[pl.ds(base, 128), :] = value[:, 0:128]
        packed[pl.ds(base + 128, 128), :] = value[:, 128:256]
        packed[pl.ds(base + 256, 64), :] = jnp.concatenate(
            [value[0:64, 256:320], value[64:128, 256:320]], axis=1
        )

    def a2a_start(way, chunk, source, target):
        depth = len(CHUNKS[chunk]) * 10
        base = STARTS[chunk] * 10 * CLIPS
        for peer in range(CLIPS):
            source[peer] = packed[pl.ds(base + peer, depth, stride=CLIPS), :].astype(BF16)
        target[clip] = source[clip]
        for i in range(1, CLIPS):
            peer = wrap(clip + i, CLIPS)
            pltpu.make_async_remote_copy(
                src_ref=source.at[peer],
                dst_ref=target.at[clip],
                send_sem=a2a_send_sem.at[way, chunk],
                recv_sem=a2a_recv_sem.at[way, chunk],
                device_id={"clip": peer},
                device_id_type=MESH,
            ).start()

    def a2a_finish(way, chunk, source, target):
        depth = len(CHUNKS[chunk]) * 10
        batch_wait(target, CLIPS - 1, a2a_recv_sem.at[way, chunk])
        for peer in range(CLIPS):
            spread[pl.ds(peer * 32, depth), :] = target[peer].astype(F32)
        return [unpack_row(q) for q in range(len(CHUNKS[chunk]))]

    def a2a_drain(way, chunk, source, target):
        batch_wait(source, CLIPS - 1, a2a_send_sem.at[way, chunk])

    def unpack_row(q):
        def column(k):
            return spread[pl.ds(q * 10 + k, CLIPS, stride=32), :]

        left = jnp.concatenate([column(k) for k in range(4)], axis=0)
        middle = jnp.concatenate([column(4 + k) for k in range(4)], axis=0)
        tail = jnp.concatenate([column(8), column(9)], axis=0)
        right = jnp.concatenate([tail, pltpu.roll(tail, 64, 1)], axis=0)
        return jnp.concatenate([left, middle, right[:, 0:64]], axis=1)

    one_live = length[0] == 1
    sends, recvs = (send_0, send_1), (recv_0, recv_1)
    back_sends, back_recvs = (back_send_0, back_send_1), (back_recv_0, back_recv_1)

    for chunk in range(2):
        if chunk == 1:
            halo_finish(1)
            fill_edges(1, scale, shift)
        total = convolve(chunk, w_two)
        for q, row in enumerate(CHUNKS[chunk]):
            halves = []
            for f in range(2):
                span = slice((2 * q + f) * W, (2 * q + f + 1) * W)
                value = lat[f, pl.ds(row * W, W), :].astype(F32) + total[span]
                halves.append(jnp.where(one_live, DEAD, value) if f == 1 else value)
            pack_row(STARTS[chunk] + q, jnp.concatenate(halves, axis=0))
        a2a_start(0, chunk, sends[chunk], recvs[chunk])

    for load in loads[8:]:
        load.wait()
    exchange_drain(1)

    lane = lax.broadcasted_iota(jnp.int32, (128, 128), 1)
    line = lax.broadcasted_iota(jnp.int32, (128, 128), 0)
    lane_clip, lane_cell, lane_slot = lane & 31, (lane >> 5) & 1, lane >> 6
    line_clip, line_cell = line & 31, (line >> 5) & 1
    lane_frame = lane_clip * 2 + lane_slot
    shared = jnp.zeros((128, 128), F32)
    for j in range(8):
        shared = shared + jnp.where(lane_frame == context[j], 1.0, 0.0)
    low_half = lane < HEAD_DIM
    clip_row = lax.broadcasted_iota(jnp.int32, (CLIPS, C), 0)

    for chunk in range(2):
        rows = len(CHUNKS[chunk])
        blocks = a2a_finish(0, chunk, sends[chunk], recvs[chunk])
        dead = jnp.broadcast_to(blocks[0][64:96, 0:1], (CLIPS, 128)) > DEAD_LIMIT
        dead_wide = jnp.broadcast_to(blocks[0][64:96, 0:1], (CLIPS, C)) > DEAD_LIMIT
        dead_f = jnp.where(dead, 1.0, 0.0)
        dead_lane = jnp.sum(
            jnp.where(
                lax.broadcasted_iota(jnp.int32, (CLIPS, 128), 0)
                == (lax.broadcasted_iota(jnp.int32, (CLIPS, 128), 1) & 31),
                dead_f,
                0.0,
            ),
            axis=0,
            keepdims=True,
        )
        live_key = 1.0 - jnp.where(lane_slot == 1, jnp.broadcast_to(dead_lane, (128, 128)), 0.0)
        weight = jnp.where(
            lane_cell == line_cell,
            jnp.where(lane_clip == line_clip, live_key, 0.0) + shared,
            0.0,
        )
        visible = weight > 0.0
        weight2 = jnp.concatenate([weight, weight], axis=1)
        visible2 = jnp.concatenate([visible, visible], axis=1)

        sources = []
        for q in range(rows):
            x = jnp.where(blocks[q] > DEAD_LIMIT, 0.0, blocks[q])
            sources.append(x)
            moving = rounded(silu(x))
            before, after = [None] * 4, [None] * 4
            for cell in range(2):
                m0 = moving[cell * 32 : cell * 32 + 32]
                m1 = moving[64 + cell * 32 : 96 + cell * 32]
                final = jnp.where(dead_wide, m0, m1)
                prior = jnp.where(clip_row == 0, 0.0, pltpu.roll(final, 1, 0))
                later = jnp.where(clip_row == CLIPS - 1, 0.0, pltpu.roll(m0, CLIPS - 1, 0))
                before[cell], before[2 + cell] = prior, m0
                after[cell], after[2 + cell] = jnp.where(dead_wide, later, m1), later
            taps[0, pl.ds(q * 128, 128), :] = jnp.concatenate(
                [
                    jnp.concatenate(before, axis=0).astype(BF16),
                    moving.astype(BF16),
                    jnp.concatenate(after, axis=0).astype(BF16),
                ],
                axis=1,
            )
        source = jnp.concatenate(sources, axis=0)
        res_two = rounded(source + dot(taps[0, pl.ds(0, rows * 128), :], w_time[...]))
        centre = jnp.mean(res_two, axis=1, keepdims=True)
        offset = res_two - centre
        variance = jnp.mean(offset * offset, axis=1, keepdims=True)
        normed = (offset * lax.rsqrt(variance + EPS) * gain_attn[...].reshape(1, C)).astype(BF16)
        q_all = dot(normed, w_qkv[:, 0:C]).astype(BF16)
        k_all = dot(normed, w_qkv[:, C : 2 * C]).astype(BF16)
        v_all = dot(normed, w_qkv[:, 2 * C : 3 * C]).astype(BF16)
        zero = jnp.zeros((128, 128), BF16)
        attended = []
        for q in range(rows):
            span = slice(q * 128, (q + 1) * 128)
            pieces = []
            for pair in range(2):
                cols = slice(pair * 128, (pair + 1) * 128)
                queries, keys, values = q_all[span, cols], k_all[span, cols], v_all[span, cols]
                keys2 = jnp.concatenate(
                    [jnp.where(low_half, keys, zero), jnp.where(low_half, zero, keys)], axis=0
                )
                values2 = jnp.concatenate(
                    [jnp.where(low_half, values, zero), jnp.where(low_half, zero, values)], axis=0
                )
                scores = lax.dot_general(
                    queries, keys2, (((1,), (1,)), ((), ())), preferred_element_type=F32
                ) * (HEAD_DIM**-0.5)
                scores = jnp.where(visible2, scores, MASKED)
                top = jnp.concatenate(
                    [
                        jnp.broadcast_to(
                            jnp.max(scores[:, i * 128 : (i + 1) * 128], axis=1, keepdims=True),
                            (128, 128),
                        )
                        for i in range(2)
                    ],
                    axis=1,
                )
                grown = jnp.exp(scores - top) * weight2
                norm = jnp.where(
                    low_half,
                    jnp.broadcast_to(jnp.sum(grown[:, 0:128], axis=1, keepdims=True), (128, 128)),
                    jnp.broadcast_to(jnp.sum(grown[:, 128:256], axis=1, keepdims=True), (128, 128)),
                )
                pieces.append((dot(grown.astype(BF16), values2) / norm).astype(BF16))
            cols = slice(256, 320)
            scores = lax.dot_general(
                q_all[span, cols], k_all[span, cols], (((1,), (1,)), ((), ())),
                preferred_element_type=F32,
            ) * (HEAD_DIM**-0.5)
            scores = jnp.where(visible, scores, MASKED)
            grown = jnp.exp(scores - jnp.max(scores, axis=1, keepdims=True)) * weight
            norm = jnp.sum(grown, axis=1, keepdims=True)
            pieces.append((dot(grown.astype(BF16), v_all[span, cols]) / norm).astype(BF16))
            attended.append(jnp.concatenate(pieces, axis=1))
        result = res_two + dot(jnp.concatenate(attended, axis=0), w_out[...])
        for q in range(rows):
            block = result[q * 128 : (q + 1) * 128]
            parts = [block[0:64]]
            for cell in range(2):
                parts.append(jnp.where(dead_wide, 0.0, block[64 + cell * 32 : 96 + cell * 32]))
            pack_row(STARTS[chunk] + q, jnp.concatenate(parts, axis=0))
        a2a_start(1, chunk, back_sends[chunk], back_recvs[chunk])

    for chunk in range(2):
        a2a_drain(0, chunk, sends[chunk], recvs[chunk])
    for chunk in range(2):
        blocks = a2a_finish(1, chunk, back_sends[chunk], back_recvs[chunk])
        for q, row in enumerate(CHUNKS[chunk]):
            for f in range(2):
                out[f, pl.ds(row * W, W), :] = blocks[q][f * 64 : (f + 1) * 64].astype(BF16)
    for chunk in range(2):
        a2a_drain(1, chunk, back_sends[chunk], back_recvs[chunk])


def in_hbm(x):
    return pltpu.with_memory_space_constraint(x, pltpu.HBM)


def local(
    latents, lengths, context, gain_first, conv_first, gain_second, conv_second,
    time_weight, attn_gain, w_qkv, w_out,
):
    vmem = pl.BlockSpec(memory_space=pltpu.VMEM)
    hbm = pl.BlockSpec(memory_space=pltpu.HBM)

    def messages(chunk):
        return pltpu.VMEM((CLIPS, len(CHUNKS[chunk]) * 10, 128), BF16)

    result = pl.pallas_call(
        kernel,
        out_shape=jax.ShapeDtypeStruct((2, ROWS * W, C), BF16),
        in_specs=[hbm] * 11,
        out_specs=vmem,
        scratch_shapes=[
            pltpu.VMEM((2, ROWS * W, C), BF16),
            pltpu.SMEM((1,), jnp.int32),
            pltpu.SMEM((8,), jnp.int32),
            pltpu.VMEM((C,), F32),
            pltpu.VMEM((C,), F32),
            pltpu.VMEM((C,), F32),
            pltpu.VMEM((3, 3 * C, C), BF16),
            pltpu.VMEM((3, 3 * C, C), BF16),
            pltpu.VMEM((3 * C, C), BF16),
            pltpu.VMEM((C, 3 * C), BF16),
            pltpu.VMEM((C, C), BF16),
            pltpu.VMEM((2, (ROWS + 2) * W, 3 * C), BF16),
            pltpu.VMEM((2, ROWS * W, C), BF16),
            pltpu.VMEM((2, 2, 5, W, 128), BF16),
            pltpu.VMEM((2, 2, 5, W, 128), BF16),
            pltpu.VMEM((C, C), BF16),
            pltpu.VMEM((2, 4, C), F32),
            pltpu.VMEM((2, TILES, 4, C), F32),
            pltpu.VMEM((ROWS * 10 * CLIPS, 128), F32),
            pltpu.VMEM((CLIPS * 32, 128), F32),
            messages(0), messages(1), messages(0), messages(1),
            messages(0), messages(1), messages(0), messages(1),
            pltpu.SemaphoreType.DMA((11,)),
            pltpu.SemaphoreType.DMA((2, 2)),
            pltpu.SemaphoreType.DMA((2, 2)),
            pltpu.SemaphoreType.DMA((2,)),
            pltpu.SemaphoreType.DMA((2,)),
            pltpu.SemaphoreType.DMA((2, 2)),
            pltpu.SemaphoreType.DMA((2, 2)),
        ],
        compiler_params=pltpu.CompilerParams(
            collective_id=0, has_side_effects=True, vmem_limit_bytes=48 << 20
        ),
        name="block",
    )(
        in_hbm(latents.reshape(2, ROWS * W, C)),
        lengths,
        in_hbm(context),
        in_hbm(gain_first),
        in_hbm(gain_second),
        in_hbm(attn_gain),
        in_hbm(conv_first.reshape(3, 3 * C, C)),
        in_hbm(conv_second.reshape(3, 3 * C, C)),
        in_hbm(time_weight.reshape(3 * C, C)),
        in_hbm(w_qkv),
        in_hbm(w_out),
    )
    return result.reshape(2, ROWS, W, C)


def solution(mesh):
    placed = (P("clip", "tile", None, None), P("clip"), P(), P(), P(), P(), P(), P(), P(), P(), P())
    return jax.shard_map(
        local, mesh=mesh, in_specs=placed, out_specs=P("clip", "tile", None, None), check_vma=False
    )
```

```python
import jax
import jax.numpy as jnp
from jax import lax
from jax.experimental import pallas as pl
from jax.experimental.pallas import tpu as pltpu
from jax.sharding import PartitionSpec as P

MESH = pl.DeviceIdType.MESH
F32 = jnp.float32
BF16 = jnp.bfloat16

C = 320
HEAD_DIM = 64
HEADS = 5
GROUP_WIDTH = 10
H = 40
W = 64
ROWS = 5
CLIPS = 32
TILES = 8
COUNT = H * W * GROUP_WIDTH
EPS = 1e-05
MASKED = -1e30
DEAD = 1e30
DEAD_LIMIT = 1e20
CHUNKS = ((1, 2, 3), (0, 4))
STARTS = (0, 3)


def wrap(value, size):
    return jnp.where(value >= size, value - size, value)


def dot(a, b):
    return jnp.dot(a, b, preferred_element_type=F32)


def silu(y):
    half = 0.5 * y
    return half + half * jnp.tanh(half)


def rounded(v):
    return v.astype(BF16).astype(F32)


def channel_sums(frames):
    sums = [jnp.sum(v, axis=0, keepdims=True) for v in frames]
    squares = [jnp.sum(v * v, axis=0, keepdims=True) for v in frames]
    return jnp.concatenate(sums + squares, axis=0)


def kernel(
    lat_hbm, length_hbm, context_hbm, gain_one_hbm, gain_two_hbm, gain_attn_hbm,
    w_one_hbm, w_two_hbm, w_time_hbm, w_qkv_hbm, w_out_hbm,
    out,
    lat, length, context, gain_one, gain_two, gain_attn, w_one, w_two, w_time, w_qkv, w_out,
    taps, hid, halo_send, halo, member, stat_send, stat_recv, packed, qkv, masks,
    send_0, send_1, recv_0, recv_1, back_send_0, back_send_1, back_recv_0, back_recv_1,
    load_sem, halo_send_sem, halo_recv_sem, stat_send_sem, stat_recv_sem,
    a2a_send_sem, a2a_recv_sem,
):
    clip = lax.axis_index("clip")
    tile = lax.axis_index("tile")
    tile_up, tile_down = wrap(tile + TILES - 1, TILES), wrap(tile + 1, TILES)

    loads = [
        pltpu.make_async_copy(source, target, load_sem.at[i])
        for i, (source, target) in enumerate(
            (
                (lat_hbm, lat),
                (length_hbm, length),
                (context_hbm, context),
                (gain_one_hbm, gain_one),
                (gain_two_hbm, gain_two),
                (gain_attn_hbm, gain_attn),
                (w_one_hbm, w_one),
                (w_two_hbm, w_two),
                (w_time_hbm, w_time),
                (w_qkv_hbm, w_qkv),
                (w_out_hbm, w_out),
            )
        )
    ]
    for load in loads:
        load.start()

    barrier = pltpu.get_barrier_semaphore()

    for i in range(1, CLIPS):
        pl.semaphore_signal(
            barrier, inc=1, device_id={"clip": wrap(clip + i, CLIPS)}, device_id_type=MESH
        )
    for i in range(1, TILES):
        pl.semaphore_signal(
            barrier, inc=1, device_id={"tile": wrap(tile + i, TILES)}, device_id_type=MESH
        )

    rows = lax.broadcasted_iota(jnp.int32, (C, C), 0)
    cols = lax.broadcasted_iota(jnp.int32, (C, C), 1)
    member[...] = jnp.where(((rows * 6554) >> 16) == ((cols * 6554) >> 16), 1.0, 0.0).astype(BF16)

    def pack_halo(phase, source):
        for way, start in enumerate(((ROWS - 1) * W, 0)):
            span = pl.ds(start, W)
            for f in range(2):
                halo_send[phase, way, 2 * f] = source[f, span, 0:128]
                halo_send[phase, way, 2 * f + 1] = source[f, span, 128:256]
            halo_send[phase, way, 4] = jnp.concatenate(
                [source[0, span, 256:320], source[1, span, 256:320]], axis=1
            )

    for load in loads[:6]:
        load.wait()
    pack_halo(0, lat)
    first = channel_sums([lat[0].astype(F32), lat[1].astype(F32)])
    stat_send[0] = first
    pl.semaphore_wait(barrier, TILES - 1 + CLIPS - 1)

    def halo_copies(phase):
        return [
            pltpu.make_async_remote_copy(
                src_ref=halo_send.at[phase, way],
                dst_ref=halo.at[phase, way],
                send_sem=halo_send_sem.at[phase, way],
                recv_sem=halo_recv_sem.at[phase, way],
                device_id={"tile": peer},
                device_id_type=MESH,
            )
            for way, peer in enumerate((tile_down, tile_up))
        ]

    def stats_start(phase):
        for i in range(1, TILES):
            pltpu.make_async_remote_copy(
                src_ref=stat_send.at[phase],
                dst_ref=stat_recv.at[phase, tile],
                send_sem=stat_send_sem.at[phase],
                recv_sem=stat_recv_sem.at[phase],
                device_id={"tile": wrap(tile + i, TILES)},
                device_id_type=MESH,
            ).start()

    def batch_wait(buffer, count, sem):
        span = buffer.at[pl.ds(0, count)]
        pltpu.make_async_copy(span, span, sem).wait()

    def halo_start(phase):
        for copy in halo_copies(phase):
            copy.start()

    def halo_finish(phase):
        for copy in halo_copies(phase):
            copy.wait_recv()

    def stats_finish(phase, own, gain):
        stat_recv[phase, tile] = own

        batch_wait(stat_recv.at[phase], TILES - 1, stat_recv_sem.at[phase])
        total = stat_recv[phase, 0]
        for i in range(1, TILES):
            total = total + stat_recv[phase, i]
        top = total.astype(BF16)
        rest = total - top.astype(F32)
        mid = rest.astype(BF16)
        low = (rest - mid.astype(F32)).astype(BF16)
        grouped = dot(jnp.concatenate([top, mid, low], axis=0), member[...])
        grouped = ((grouped[8:12] + grouped[4:8]) + grouped[0:4]) * (1.0 / COUNT)
        centre = grouped[0:2]
        variance = grouped[2:4] - centre * centre
        scale = lax.rsqrt(variance + EPS) * gain[...].reshape(1, C)
        return scale, -centre * scale

    def exchange_drain(phase):
        batch_wait(stat_recv.at[phase], TILES - 1, stat_send_sem.at[phase])
        for copy in halo_copies(phase):
            copy.wait_send()

    def put_taps(f, start, rows, value, scale, shift, keep=None):
        a = silu(value.astype(F32) * scale + shift)
        if keep is not None:
            a = jnp.where(keep, a, 0.0)
        column = lax.broadcasted_iota(jnp.int32, (rows * W, C), 0) & (W - 1)
        before = jnp.where(column == 0, 0.0, pltpu.roll(a, 1, 0))
        after = jnp.where(column == W - 1, 0.0, pltpu.roll(a, rows * W - 1, 0))
        taps[f, pl.ds(start, rows * W), :] = jnp.concatenate(
            [before.astype(BF16), a.astype(BF16), after.astype(BF16)], axis=1
        )

    def fill_own(source, scale, shift):
        for f in range(2):
            put_taps(f, W, ROWS, source[f], scale[f : f + 1], shift[f : f + 1])

    def fill_edges(phase, scale, shift):
        for way, (start, keep) in enumerate(((0, tile > 0), ((ROWS + 1) * W, tile < TILES - 1))):
            for f in range(2):
                value = jnp.concatenate(
                    [
                        halo[phase, way, 2 * f],
                        halo[phase, way, 2 * f + 1],
                        halo[phase, way, 4][:, f * 64 : (f + 1) * 64],
                    ],
                    axis=1,
                )
                put_taps(f, start, 1, value, scale[f : f + 1], shift[f : f + 1], keep)

    def convolve(chunk, weights):
        total = None
        for a in range(3):
            lines = [
                taps[f, pl.ds((row + a) * W, W), :] for row in CHUNKS[chunk] for f in range(2)
            ]
            term = dot(jnp.concatenate(lines, axis=0), weights[a])
            total = term if total is None else total + term
        return total

    def first_convolution(chunk):
        value = convolve(chunk, w_one).astype(BF16)
        sums = []
        for q, row in enumerate(CHUNKS[chunk]):
            for f in range(2):
                hid[f, pl.ds(row * W, W), :] = value[(2 * q + f) * W : (2 * q + f + 1) * W]
        wide = value.astype(F32)
        for f in range(2):
            parts = [wide[(2 * q + f) * W : (2 * q + f + 1) * W] for q in range(len(CHUNKS[chunk]))]
            sums.append(jnp.concatenate(parts, axis=0))
        return channel_sums(sums)

    stats_start(0)
    halo_start(0)
    for load in loads[6:]:
        load.wait()
    for i in range(3):
        qkv[i] = w_qkv[:, i * C : (i + 1) * C]
    scale, shift = stats_finish(0, first, gain_one)
    fill_own(lat, scale, shift)
    second = first_convolution(0)
    halo_finish(0)
    fill_edges(0, scale, shift)
    second = second + first_convolution(1)
    stat_send[1] = second
    pack_halo(1, hid)

    stats_start(1)
    halo_start(1)
    exchange_drain(0)
    scale, shift = stats_finish(1, second, gain_two)
    fill_own(hid, scale, shift)

    def pack_row(r, value):
        base = r * 10 * CLIPS
        packed[pl.ds(base, 128), :] = value[:, 0:128]
        packed[pl.ds(base + 128, 128), :] = value[:, 128:256]
        packed[pl.ds(base + 256, 64), :] = jnp.concatenate(
            [value[0:64, 256:320], value[64:128, 256:320]], axis=1
        )

    def a2a_start(way, chunk, source, target):
        depth = len(CHUNKS[chunk]) * 10
        base = STARTS[chunk] * 10 * CLIPS
        block = packed[pl.ds(base, depth * CLIPS), :].reshape(depth, CLIPS, 128)
        source[...] = jnp.swapaxes(block, 0, 1).astype(BF16)
        target[clip] = source[clip]
        for i in range(1, CLIPS):
            peer = wrap(clip + i, CLIPS)
            pltpu.make_async_remote_copy(
                src_ref=source.at[peer],
                dst_ref=target.at[clip],
                send_sem=a2a_send_sem.at[way, chunk],
                recv_sem=a2a_recv_sem.at[way, chunk],
                device_id={"clip": peer},
                device_id_type=MESH,
            ).start()

    def a2a_finish(way, chunk, source, target):
        batch_wait(target, CLIPS - 1, a2a_recv_sem.at[way, chunk])
        block = jnp.swapaxes(target[...].astype(F32), 0, 1)
        return [unpack_row(block[q * 10 : q * 10 + 10]) for q in range(len(CHUNKS[chunk]))]

    def a2a_drain(way, chunk, source, target):
        batch_wait(source, CLIPS - 1, a2a_send_sem.at[way, chunk])

    def unpack_row(block):
        left, middle = block[0:4].reshape(128, 128), block[4:8].reshape(128, 128)
        tail = block[8:10].reshape(64, 128)
        right = jnp.concatenate([tail, pltpu.roll(tail, 64, 1)], axis=0)
        return jnp.concatenate([left, middle, right[:, 0:64]], axis=1)

    one_live = length[0] == 1
    sends, recvs = (send_0, send_1), (recv_0, recv_1)
    back_sends, back_recvs = (back_send_0, back_send_1), (back_recv_0, back_recv_1)

    for chunk in range(2):
        if chunk == 1:
            halo_finish(1)
            fill_edges(1, scale, shift)
        total = convolve(chunk, w_two)
        for q, row in enumerate(CHUNKS[chunk]):
            halves = []
            for f in range(2):
                span = slice((2 * q + f) * W, (2 * q + f + 1) * W)
                value = lat[f, pl.ds(row * W, W), :].astype(F32) + total[span]
                halves.append(jnp.where(one_live, DEAD, value) if f == 1 else value)
            pack_row(STARTS[chunk] + q, jnp.concatenate(halves, axis=0))
        a2a_start(0, chunk, sends[chunk], recvs[chunk])

    exchange_drain(1)

    lane = lax.broadcasted_iota(jnp.int32, (128, 128), 1)
    line = lax.broadcasted_iota(jnp.int32, (128, 128), 0)
    lane_clip, lane_cell, lane_slot = lane & 31, (lane >> 5) & 1, lane >> 6
    line_clip, line_cell = line & 31, (line >> 5) & 1
    lane_frame = lane_clip * 2 + lane_slot
    shared = jnp.zeros((128, 128), F32)
    for j in range(8):
        shared = shared + jnp.where(lane_frame == context[j], 1.0, 0.0)
    low_half = lane < HEAD_DIM
    clip_row = lax.broadcasted_iota(jnp.int32, (CLIPS, C), 0)

    for chunk in range(2):
        rows = len(CHUNKS[chunk])
        blocks = a2a_finish(0, chunk, sends[chunk], recvs[chunk])
        if chunk == 0:
            dead = jnp.broadcast_to(blocks[0][64:96, 0:1], (CLIPS, 128)) > DEAD_LIMIT
            dead_wide = jnp.broadcast_to(blocks[0][64:96, 0:1], (CLIPS, C)) > DEAD_LIMIT
            dead_f = jnp.where(dead, 1.0, 0.0)
            dead_lane = jnp.sum(
                jnp.where(
                    lax.broadcasted_iota(jnp.int32, (CLIPS, 128), 0)
                    == (lax.broadcasted_iota(jnp.int32, (CLIPS, 128), 1) & 31),
                    dead_f,
                    0.0,
                ),
                axis=0,
                keepdims=True,
            )
            live_key = 1.0 - jnp.where(lane_slot == 1, jnp.broadcast_to(dead_lane, (128, 128)), 0.0)
            weight = jnp.where(
                lane_cell == line_cell,
                jnp.where(lane_clip == line_clip, live_key, 0.0) + shared,
                0.0,
            )
            masks[0] = weight
            masks[1] = jnp.where(weight > 0.0, 0.0, MASKED)

        sources = []
        for q in range(rows):
            x = jnp.where(blocks[q] > DEAD_LIMIT, 0.0, blocks[q])
            sources.append(x)
            moving = rounded(silu(x))
            before, after = [None] * 4, [None] * 4
            for cell in range(2):
                m0 = moving[cell * 32 : cell * 32 + 32]
                m1 = moving[64 + cell * 32 : 96 + cell * 32]
                final = jnp.where(dead_wide, m0, m1)
                prior = jnp.where(clip_row == 0, 0.0, pltpu.roll(final, 1, 0))
                later = jnp.where(clip_row == CLIPS - 1, 0.0, pltpu.roll(m0, CLIPS - 1, 0))
                before[cell], before[2 + cell] = prior, m0
                after[cell], after[2 + cell] = jnp.where(dead_wide, later, m1), later
            taps[0, pl.ds(q * 128, 128), :] = jnp.concatenate(
                [
                    jnp.concatenate(before, axis=0).astype(BF16),
                    moving.astype(BF16),
                    jnp.concatenate(after, axis=0).astype(BF16),
                ],
                axis=1,
            )
        source = jnp.concatenate(sources, axis=0)
        res_two = rounded(source + dot(taps[0, pl.ds(0, rows * 128), :], w_time[...]))
        centre = jnp.mean(res_two, axis=1, keepdims=True)
        offset = res_two - centre
        variance = jnp.mean(offset * offset, axis=1, keepdims=True)
        normed = (offset * lax.rsqrt(variance + EPS) * gain_attn[...].reshape(1, C)).astype(BF16)
        q_all = (dot(normed, qkv[0]) * (HEAD_DIM**-0.5)).astype(BF16)
        k_all = dot(normed, qkv[1]).astype(BF16)
        v_all = dot(normed, qkv[2]).astype(BF16)
        zero = jnp.zeros((128, 128), BF16)
        attended = []
        for q in range(rows):
            span = slice(q * 128, (q + 1) * 128)
            pieces = []
            for pair in range(2):
                cols = slice(pair * 128, (pair + 1) * 128)
                queries, keys, values = q_all[span, cols], k_all[span, cols], v_all[span, cols]
                keys2 = jnp.concatenate(
                    [jnp.where(low_half, keys, zero), jnp.where(low_half, zero, keys)], axis=0
                )
                values2 = jnp.concatenate(
                    [jnp.where(low_half, values, zero), jnp.where(low_half, zero, values)], axis=0
                )
                scores = lax.dot_general(
                    queries, keys2, (((1,), (1,)), ((), ())), preferred_element_type=F32
                )
                grown, norms = [], []
                for i in range(2):
                    part = scores[:, i * 128 : (i + 1) * 128] + masks[1]
                    part = jnp.exp(part - jnp.max(part, axis=1, keepdims=True)) * masks[0]
                    norms.append(jnp.broadcast_to(jnp.sum(part, axis=1, keepdims=True), (128, 128)))
                    grown.append(part.astype(BF16))
                norm = jnp.where(low_half, norms[0], norms[1])
                grown = jnp.concatenate(grown, axis=1)
                pieces.append((dot(grown, values2) / norm).astype(BF16))
            cols = slice(256, 320)
            scores = lax.dot_general(
                q_all[span, cols], k_all[span, cols], (((1,), (1,)), ((), ())),
                preferred_element_type=F32,
            )
            scores = scores + masks[1]
            grown = jnp.exp(scores - jnp.max(scores, axis=1, keepdims=True)) * masks[0]
            norm = jnp.sum(grown, axis=1, keepdims=True)
            pieces.append((dot(grown.astype(BF16), v_all[span, cols]) / norm).astype(BF16))
            attended.append(jnp.concatenate(pieces, axis=1))
        result = res_two + dot(jnp.concatenate(attended, axis=0), w_out[...])
        for q in range(rows):
            block = result[q * 128 : (q + 1) * 128]
            parts = [block[0:64]]
            for cell in range(2):
                parts.append(jnp.where(dead_wide, 0.0, block[64 + cell * 32 : 96 + cell * 32]))
            pack_row(STARTS[chunk] + q, jnp.concatenate(parts, axis=0))
        a2a_start(1, chunk, back_sends[chunk], back_recvs[chunk])

    for chunk in range(2):
        a2a_drain(0, chunk, sends[chunk], recvs[chunk])
    for chunk in range(2):
        blocks = a2a_finish(1, chunk, back_sends[chunk], back_recvs[chunk])
        for q, row in enumerate(CHUNKS[chunk]):
            for f in range(2):
                out[f, pl.ds(row * W, W), :] = blocks[q][f * 64 : (f + 1) * 64].astype(BF16)
    for chunk in range(2):
        a2a_drain(1, chunk, back_sends[chunk], back_recvs[chunk])


def in_hbm(x):
    return pltpu.with_memory_space_constraint(x, pltpu.HBM)


def local(
    latents, lengths, context, gain_first, conv_first, gain_second, conv_second,
    time_weight, attn_gain, w_qkv, w_out,
):
    vmem = pl.BlockSpec(memory_space=pltpu.VMEM)
    hbm = pl.BlockSpec(memory_space=pltpu.HBM)

    def messages(chunk):
        return pltpu.VMEM((CLIPS, len(CHUNKS[chunk]) * 10, 128), BF16)

    result = pl.pallas_call(
        kernel,
        out_shape=jax.ShapeDtypeStruct((2, ROWS * W, C), BF16),
        in_specs=[hbm] * 11,
        out_specs=vmem,
        scratch_shapes=[
            pltpu.VMEM((2, ROWS * W, C), BF16),
            pltpu.SMEM((1,), jnp.int32),
            pltpu.SMEM((8,), jnp.int32),
            pltpu.VMEM((C,), F32),
            pltpu.VMEM((C,), F32),
            pltpu.VMEM((C,), F32),
            pltpu.VMEM((3, 3 * C, C), BF16),
            pltpu.VMEM((3, 3 * C, C), BF16),
            pltpu.VMEM((3 * C, C), BF16),
            pltpu.VMEM((C, 3 * C), BF16),
            pltpu.VMEM((C, C), BF16),
            pltpu.VMEM((2, (ROWS + 2) * W, 3 * C), BF16),
            pltpu.VMEM((2, ROWS * W, C), BF16),
            pltpu.VMEM((2, 2, 5, W, 128), BF16),
            pltpu.VMEM((2, 2, 5, W, 128), BF16),
            pltpu.VMEM((C, C), BF16),
            pltpu.VMEM((2, 4, C), F32),
            pltpu.VMEM((2, TILES, 4, C), F32),
            pltpu.VMEM((ROWS * 10 * CLIPS, 128), F32),
            pltpu.VMEM((3, C, C), BF16),
            pltpu.VMEM((2, 128, 128), F32),
            messages(0), messages(1), messages(0), messages(1),
            messages(0), messages(1), messages(0), messages(1),
            pltpu.SemaphoreType.DMA((11,)),
            pltpu.SemaphoreType.DMA((2, 2)),
            pltpu.SemaphoreType.DMA((2, 2)),
            pltpu.SemaphoreType.DMA((2,)),
            pltpu.SemaphoreType.DMA((2,)),
            pltpu.SemaphoreType.DMA((2, 2)),
            pltpu.SemaphoreType.DMA((2, 2)),
        ],
        compiler_params=pltpu.CompilerParams(
            collective_id=0, has_side_effects=True, vmem_limit_bytes=48 << 20
        ),
        name="block",
    )(
        in_hbm(latents.reshape(2, ROWS * W, C)),
        lengths,
        in_hbm(context),
        in_hbm(gain_first),
        in_hbm(gain_second),
        in_hbm(attn_gain),
        in_hbm(conv_first.reshape(3, 3 * C, C)),
        in_hbm(conv_second.reshape(3, 3 * C, C)),
        in_hbm(time_weight.reshape(3 * C, C)),
        in_hbm(w_qkv),
        in_hbm(w_out),
    )
    return result.reshape(2, ROWS, W, C)


def solution(mesh):
    placed = (P("clip", "tile", None, None), P("clip"), P(), P(), P(), P(), P(), P(), P(), P(), P())
    return jax.shard_map(
        local, mesh=mesh, in_specs=placed, out_specs=P("clip", "tile", None, None), check_vma=False
    )
```

```python
import jax
import jax.numpy as jnp
from jax import lax
from jax.experimental import pallas as pl
from jax.experimental.pallas import tpu as pltpu
from jax.sharding import PartitionSpec as P

MESH = pl.DeviceIdType.MESH
F32 = jnp.float32
BF16 = jnp.bfloat16

C = 320
HEAD_DIM = 64
HEADS = 5
GROUP_WIDTH = 10
H = 40
W = 64
ROWS = 5
CLIPS = 32
TILES = 8
COUNT = H * W * GROUP_WIDTH
EPS = 1e-05
MASKED = -1e30
DEAD = 1e30
DEAD_LIMIT = 1e20
CHUNKS = ((1, 2), (3, 0, 4))
STARTS = (0, 2)


def wrap(value, size):
    return jnp.where(value >= size, value - size, value)


def dot(a, b):
    return jnp.dot(a, b, preferred_element_type=F32)


def silu(y):
    half = 0.5 * y
    return half + half * jnp.tanh(half)


def rounded(v):
    return v.astype(BF16).astype(F32)


def channel_sums(frames):
    sums = [jnp.sum(v, axis=0, keepdims=True) for v in frames]
    squares = [jnp.sum(v * v, axis=0, keepdims=True) for v in frames]
    return jnp.concatenate(sums + squares, axis=0)


def kernel(
    lat_hbm, length_hbm, context_hbm, gain_one_hbm, gain_two_hbm, gain_attn_hbm,
    w_one_hbm, w_two_hbm, w_time_hbm, w_qkv_hbm, w_out_hbm,
    out,
    lat, length, context, gain_one, gain_two, gain_attn, w_one, w_two, w_time, w_qkv, w_out,
    taps, hid, halo_send, halo, member, stat_send, stat_recv, packed, qkv, masks,
    send_0, send_1, recv_0, recv_1, back_send_0, back_send_1, back_recv_0, back_recv_1,
    load_sem, halo_send_sem, halo_recv_sem, stat_send_sem, stat_recv_sem,
    a2a_send_sem, a2a_recv_sem,
):
    clip = lax.axis_index("clip")
    tile = lax.axis_index("tile")
    tile_up, tile_down = wrap(tile + TILES - 1, TILES), wrap(tile + 1, TILES)

    loads = [
        pltpu.make_async_copy(source, target, load_sem.at[i])
        for i, (source, target) in enumerate(
            (
                (lat_hbm, lat),
                (length_hbm, length),
                (context_hbm, context),
                (gain_one_hbm, gain_one),
                (gain_two_hbm, gain_two),
                (gain_attn_hbm, gain_attn),
                (w_one_hbm, w_one),
                (w_two_hbm, w_two),
                (w_time_hbm, w_time),
                (w_qkv_hbm, w_qkv),
                (w_out_hbm, w_out),
            )
        )
    ]
    for load in loads:
        load.start()

    barrier = pltpu.get_barrier_semaphore()

    for i in range(1, CLIPS):
        pl.semaphore_signal(
            barrier, inc=1, device_id={"clip": wrap(clip + i, CLIPS)}, device_id_type=MESH
        )
    for i in range(1, TILES):
        pl.semaphore_signal(
            barrier, inc=1, device_id={"tile": wrap(tile + i, TILES)}, device_id_type=MESH
        )

    rows = lax.broadcasted_iota(jnp.int32, (C, C), 0)
    cols = lax.broadcasted_iota(jnp.int32, (C, C), 1)
    member[...] = jnp.where(((rows * 6554) >> 16) == ((cols * 6554) >> 16), 1.0, 0.0).astype(BF16)

    def pack_halo(phase, source):
        for way, start in enumerate(((ROWS - 1) * W, 0)):
            span = pl.ds(start, W)
            for f in range(2):
                halo_send[phase, way, 2 * f] = source[f, span, 0:128]
                halo_send[phase, way, 2 * f + 1] = source[f, span, 128:256]
            halo_send[phase, way, 4] = jnp.concatenate(
                [source[0, span, 256:320], source[1, span, 256:320]], axis=1
            )

    for load in loads[:6]:
        load.wait()
    pack_halo(0, lat)
    first = channel_sums([lat[0].astype(F32), lat[1].astype(F32)])
    stat_send[0] = first
    pl.semaphore_wait(barrier, TILES - 1 + CLIPS - 1)

    def halo_copies(phase):
        return [
            pltpu.make_async_remote_copy(
                src_ref=halo_send.at[phase, way],
                dst_ref=halo.at[phase, way],
                send_sem=halo_send_sem.at[phase, way],
                recv_sem=halo_recv_sem.at[phase, way],
                device_id={"tile": peer},
                device_id_type=MESH,
            )
            for way, peer in enumerate((tile_down, tile_up))
        ]

    def stats_start(phase):
        for i in range(1, TILES):
            pltpu.make_async_remote_copy(
                src_ref=stat_send.at[phase],
                dst_ref=stat_recv.at[phase, tile],
                send_sem=stat_send_sem.at[phase],
                recv_sem=stat_recv_sem.at[phase],
                device_id={"tile": wrap(tile + i, TILES)},
                device_id_type=MESH,
            ).start()

    def batch_wait(buffer, count, sem):
        span = buffer.at[pl.ds(0, count)]
        pltpu.make_async_copy(span, span, sem).wait()

    def halo_start(phase):
        for copy in halo_copies(phase):
            copy.start()

    def halo_finish(phase):
        for copy in halo_copies(phase):
            copy.wait_recv()

    def stats_finish(phase, own, gain):
        stat_recv[phase, tile] = own

        batch_wait(stat_recv.at[phase], TILES - 1, stat_recv_sem.at[phase])
        total = stat_recv[phase, 0]
        for i in range(1, TILES):
            total = total + stat_recv[phase, i]
        top = total.astype(BF16)
        rest = total - top.astype(F32)
        mid = rest.astype(BF16)
        low = (rest - mid.astype(F32)).astype(BF16)
        grouped = dot(jnp.concatenate([top, mid, low], axis=0), member[...])
        grouped = ((grouped[8:12] + grouped[4:8]) + grouped[0:4]) * (1.0 / COUNT)
        centre = grouped[0:2]
        variance = grouped[2:4] - centre * centre
        scale = lax.rsqrt(variance + EPS) * gain[...].reshape(1, C)
        return scale, -centre * scale

    def exchange_drain(phase):
        batch_wait(stat_recv.at[phase], TILES - 1, stat_send_sem.at[phase])
        for copy in halo_copies(phase):
            copy.wait_send()

    def put_taps(f, start, rows, value, scale, shift, keep=None):
        a = silu(value.astype(F32) * scale + shift)
        if keep is not None:
            a = jnp.where(keep, a, 0.0)
        column = lax.broadcasted_iota(jnp.int32, (rows * W, C), 0) & (W - 1)
        before = jnp.where(column == 0, 0.0, pltpu.roll(a, 1, 0))
        after = jnp.where(column == W - 1, 0.0, pltpu.roll(a, rows * W - 1, 0))
        taps[f, pl.ds(start, rows * W), :] = jnp.concatenate(
            [before.astype(BF16), a.astype(BF16), after.astype(BF16)], axis=1
        )

    def fill_own(source, scale, shift):
        for f in range(2):
            put_taps(f, W, ROWS, source[f], scale[f : f + 1], shift[f : f + 1])

    def fill_edges(phase, scale, shift):
        for way, (start, keep) in enumerate(((0, tile > 0), ((ROWS + 1) * W, tile < TILES - 1))):
            for f in range(2):
                value = jnp.concatenate(
                    [
                        halo[phase, way, 2 * f],
                        halo[phase, way, 2 * f + 1],
                        halo[phase, way, 4][:, f * 64 : (f + 1) * 64],
                    ],
                    axis=1,
                )
                put_taps(f, start, 1, value, scale[f : f + 1], shift[f : f + 1], keep)

    def convolve(chunk, weights):
        total = None
        for a in range(3):
            lines = [
                taps[f, pl.ds((row + a) * W, W), :] for row in CHUNKS[chunk] for f in range(2)
            ]
            term = dot(jnp.concatenate(lines, axis=0), weights[a])
            total = term if total is None else total + term
        return total

    def first_convolution(chunk):
        value = convolve(chunk, w_one).astype(BF16)
        sums = []
        for q, row in enumerate(CHUNKS[chunk]):
            for f in range(2):
                hid[f, pl.ds(row * W, W), :] = value[(2 * q + f) * W : (2 * q + f + 1) * W]
        wide = value.astype(F32)
        for f in range(2):
            parts = [wide[(2 * q + f) * W : (2 * q + f + 1) * W] for q in range(len(CHUNKS[chunk]))]
            sums.append(jnp.concatenate(parts, axis=0))
        return channel_sums(sums)

    stats_start(0)
    halo_start(0)
    for load in loads[6:]:
        load.wait()
    for i in range(3):
        qkv[i] = w_qkv[:, i * C : (i + 1) * C]
    scale, shift = stats_finish(0, first, gain_one)
    fill_own(lat, scale, shift)
    second = first_convolution(0)
    halo_finish(0)
    fill_edges(0, scale, shift)
    second = second + first_convolution(1)
    stat_send[1] = second
    pack_halo(1, hid)

    stats_start(1)
    halo_start(1)
    exchange_drain(0)
    scale, shift = stats_finish(1, second, gain_two)
    fill_own(hid, scale, shift)

    def pack_row(r, value):
        base = r * 10 * CLIPS
        packed[pl.ds(base, 128), :] = value[:, 0:128]
        packed[pl.ds(base + 128, 128), :] = value[:, 128:256]
        packed[pl.ds(base + 256, 64), :] = jnp.concatenate(
            [value[0:64, 256:320], value[64:128, 256:320]], axis=1
        )

    def a2a_start(way, chunk, source, target):
        depth = len(CHUNKS[chunk]) * 10
        base = STARTS[chunk] * 10 * CLIPS
        block = packed[pl.ds(base, depth * CLIPS), :].reshape(depth, CLIPS, 128)
        source[...] = jnp.swapaxes(block, 0, 1).astype(BF16)
        target[clip] = source[clip]
        for i in range(1, CLIPS):
            peer = wrap(clip + i, CLIPS)
            pltpu.make_async_remote_copy(
                src_ref=source.at[peer],
                dst_ref=target.at[clip],
                send_sem=a2a_send_sem.at[way, chunk],
                recv_sem=a2a_recv_sem.at[way, chunk],
                device_id={"clip": peer},
                device_id_type=MESH,
            ).start()

    def a2a_finish(way, chunk, source, target):
        batch_wait(target, CLIPS - 1, a2a_recv_sem.at[way, chunk])
        block = jnp.swapaxes(target[...].astype(F32), 0, 1)
        return [unpack_row(block[q * 10 : q * 10 + 10]) for q in range(len(CHUNKS[chunk]))]

    def a2a_drain(way, chunk, source, target):
        batch_wait(source, CLIPS - 1, a2a_send_sem.at[way, chunk])

    def unpack_row(block):
        left, middle = block[0:4].reshape(128, 128), block[4:8].reshape(128, 128)
        tail = block[8:10].reshape(64, 128)
        right = jnp.concatenate([tail, pltpu.roll(tail, 64, 1)], axis=0)
        return jnp.concatenate([left, middle, right[:, 0:64]], axis=1)

    one_live = length[0] == 1
    sends, recvs = (send_0, send_1), (recv_0, recv_1)
    back_sends, back_recvs = (back_send_0, back_send_1), (back_recv_0, back_recv_1)

    for chunk in range(2):
        if chunk == 1:
            halo_finish(1)
            fill_edges(1, scale, shift)
        total = convolve(chunk, w_two)
        for q, row in enumerate(CHUNKS[chunk]):
            halves = []
            for f in range(2):
                span = slice((2 * q + f) * W, (2 * q + f + 1) * W)
                value = lat[f, pl.ds(row * W, W), :].astype(F32) + total[span]
                halves.append(jnp.where(one_live, DEAD, value) if f == 1 else value)
            pack_row(STARTS[chunk] + q, jnp.concatenate(halves, axis=0))
        a2a_start(0, chunk, sends[chunk], recvs[chunk])

    exchange_drain(1)

    lane = lax.broadcasted_iota(jnp.int32, (128, 128), 1)
    line = lax.broadcasted_iota(jnp.int32, (128, 128), 0)
    lane_clip, lane_cell, lane_slot = lane & 31, (lane >> 5) & 1, lane >> 6
    line_clip, line_cell = line & 31, (line >> 5) & 1
    lane_frame = lane_clip * 2 + lane_slot
    shared = jnp.zeros((128, 128), F32)
    for j in range(8):
        shared = shared + jnp.where(lane_frame == context[j], 1.0, 0.0)
    low_half = lane < HEAD_DIM
    clip_row = lax.broadcasted_iota(jnp.int32, (CLIPS, C), 0)

    for chunk in range(2):
        rows = len(CHUNKS[chunk])
        blocks = a2a_finish(0, chunk, sends[chunk], recvs[chunk])
        if chunk == 0:
            dead = jnp.broadcast_to(blocks[0][64:96, 0:1], (CLIPS, 128)) > DEAD_LIMIT
            dead_wide = jnp.broadcast_to(blocks[0][64:96, 0:1], (CLIPS, C)) > DEAD_LIMIT
            dead_f = jnp.where(dead, 1.0, 0.0)
            dead_lane = jnp.sum(
                jnp.where(
                    lax.broadcasted_iota(jnp.int32, (CLIPS, 128), 0)
                    == (lax.broadcasted_iota(jnp.int32, (CLIPS, 128), 1) & 31),
                    dead_f,
                    0.0,
                ),
                axis=0,
                keepdims=True,
            )
            live_key = 1.0 - jnp.where(lane_slot == 1, jnp.broadcast_to(dead_lane, (128, 128)), 0.0)
            weight = jnp.where(
                lane_cell == line_cell,
                jnp.where(lane_clip == line_clip, live_key, 0.0) + shared,
                0.0,
            )
            masks[0] = weight
            masks[1] = jnp.where(weight > 0.0, 0.0, MASKED)

        sources = []
        for q in range(rows):
            x = jnp.where(blocks[q] > DEAD_LIMIT, 0.0, blocks[q])
            sources.append(x)
            moving = rounded(silu(x))
            before, after = [None] * 4, [None] * 4
            for cell in range(2):
                m0 = moving[cell * 32 : cell * 32 + 32]
                m1 = moving[64 + cell * 32 : 96 + cell * 32]
                final = jnp.where(dead_wide, m0, m1)
                prior = jnp.where(clip_row == 0, 0.0, pltpu.roll(final, 1, 0))
                later = jnp.where(clip_row == CLIPS - 1, 0.0, pltpu.roll(m0, CLIPS - 1, 0))
                before[cell], before[2 + cell] = prior, m0
                after[cell], after[2 + cell] = jnp.where(dead_wide, later, m1), later
            taps[0, pl.ds(q * 128, 128), :] = jnp.concatenate(
                [
                    jnp.concatenate(before, axis=0).astype(BF16),
                    moving.astype(BF16),
                    jnp.concatenate(after, axis=0).astype(BF16),
                ],
                axis=1,
            )
        source = jnp.concatenate(sources, axis=0)
        res_two = rounded(source + dot(taps[0, pl.ds(0, rows * 128), :], w_time[...]))
        centre = jnp.mean(res_two, axis=1, keepdims=True)
        offset = res_two - centre
        variance = jnp.mean(offset * offset, axis=1, keepdims=True)
        normed = (offset * lax.rsqrt(variance + EPS) * gain_attn[...].reshape(1, C)).astype(BF16)
        q_all = (dot(normed, qkv[0]) * (HEAD_DIM**-0.5)).astype(BF16)
        k_all = dot(normed, qkv[1]).astype(BF16)
        v_all = dot(normed, qkv[2]).astype(BF16)
        zero = jnp.zeros((128, 128), BF16)
        attended = []
        for q in range(rows):
            span = slice(q * 128, (q + 1) * 128)
            pieces = []
            for pair in range(2):
                cols = slice(pair * 128, (pair + 1) * 128)
                queries, keys, values = q_all[span, cols], k_all[span, cols], v_all[span, cols]
                keys2 = jnp.concatenate(
                    [jnp.where(low_half, keys, zero), jnp.where(low_half, zero, keys)], axis=0
                )
                values2 = jnp.concatenate(
                    [jnp.where(low_half, values, zero), jnp.where(low_half, zero, values)], axis=0
                )
                scores = lax.dot_general(
                    queries, keys2, (((1,), (1,)), ((), ())), preferred_element_type=F32
                )
                grown, norms = [], []
                for i in range(2):
                    part = scores[:, i * 128 : (i + 1) * 128] + masks[1]
                    part = jnp.exp(part - jnp.max(part, axis=1, keepdims=True)) * masks[0]
                    norms.append(jnp.broadcast_to(jnp.sum(part, axis=1, keepdims=True), (128, 128)))
                    grown.append(part.astype(BF16))
                norm = jnp.where(low_half, norms[0], norms[1])
                grown = jnp.concatenate(grown, axis=1)
                pieces.append((dot(grown, values2) / norm).astype(BF16))
            cols = slice(256, 320)
            scores = lax.dot_general(
                q_all[span, cols], k_all[span, cols], (((1,), (1,)), ((), ())),
                preferred_element_type=F32,
            )
            scores = scores + masks[1]
            grown = jnp.exp(scores - jnp.max(scores, axis=1, keepdims=True)) * masks[0]
            norm = jnp.sum(grown, axis=1, keepdims=True)
            pieces.append((dot(grown.astype(BF16), v_all[span, cols]) / norm).astype(BF16))
            attended.append(jnp.concatenate(pieces, axis=1))
        result = res_two + dot(jnp.concatenate(attended, axis=0), w_out[...])
        for q in range(rows):
            block = result[q * 128 : (q + 1) * 128]
            parts = [block[0:64]]
            for cell in range(2):
                parts.append(jnp.where(dead_wide, 0.0, block[64 + cell * 32 : 96 + cell * 32]))
            pack_row(STARTS[chunk] + q, jnp.concatenate(parts, axis=0))
        a2a_start(1, chunk, back_sends[chunk], back_recvs[chunk])

    for chunk in range(2):
        a2a_drain(0, chunk, sends[chunk], recvs[chunk])
    for chunk in range(2):
        blocks = a2a_finish(1, chunk, back_sends[chunk], back_recvs[chunk])
        for q, row in enumerate(CHUNKS[chunk]):
            for f in range(2):
                out[f, pl.ds(row * W, W), :] = blocks[q][f * 64 : (f + 1) * 64].astype(BF16)
    for chunk in range(2):
        a2a_drain(1, chunk, back_sends[chunk], back_recvs[chunk])


def in_hbm(x):
    return pltpu.with_memory_space_constraint(x, pltpu.HBM)


def local(
    latents, lengths, context, gain_first, conv_first, gain_second, conv_second,
    time_weight, attn_gain, w_qkv, w_out,
):
    vmem = pl.BlockSpec(memory_space=pltpu.VMEM)
    hbm = pl.BlockSpec(memory_space=pltpu.HBM)

    def messages(chunk):
        return pltpu.VMEM((CLIPS, len(CHUNKS[chunk]) * 10, 128), BF16)

    result = pl.pallas_call(
        kernel,
        out_shape=jax.ShapeDtypeStruct((2, ROWS * W, C), BF16),
        in_specs=[hbm] * 11,
        out_specs=vmem,
        scratch_shapes=[
            pltpu.VMEM((2, ROWS * W, C), BF16),
            pltpu.SMEM((1,), jnp.int32),
            pltpu.SMEM((8,), jnp.int32),
            pltpu.VMEM((C,), F32),
            pltpu.VMEM((C,), F32),
            pltpu.VMEM((C,), F32),
            pltpu.VMEM((3, 3 * C, C), BF16),
            pltpu.VMEM((3, 3 * C, C), BF16),
            pltpu.VMEM((3 * C, C), BF16),
            pltpu.VMEM((C, 3 * C), BF16),
            pltpu.VMEM((C, C), BF16),
            pltpu.VMEM((2, (ROWS + 2) * W, 3 * C), BF16),
            pltpu.VMEM((2, ROWS * W, C), BF16),
            pltpu.VMEM((2, 2, 5, W, 128), BF16),
            pltpu.VMEM((2, 2, 5, W, 128), BF16),
            pltpu.VMEM((C, C), BF16),
            pltpu.VMEM((2, 4, C), F32),
            pltpu.VMEM((2, TILES, 4, C), F32),
            pltpu.VMEM((ROWS * 10 * CLIPS, 128), F32),
            pltpu.VMEM((3, C, C), BF16),
            pltpu.VMEM((2, 128, 128), F32),
            messages(0), messages(1), messages(0), messages(1),
            messages(0), messages(1), messages(0), messages(1),
            pltpu.SemaphoreType.DMA((11,)),
            pltpu.SemaphoreType.DMA((2, 2)),
            pltpu.SemaphoreType.DMA((2, 2)),
            pltpu.SemaphoreType.DMA((2,)),
            pltpu.SemaphoreType.DMA((2,)),
            pltpu.SemaphoreType.DMA((2, 2)),
            pltpu.SemaphoreType.DMA((2, 2)),
        ],
        compiler_params=pltpu.CompilerParams(
            collective_id=0, has_side_effects=True, vmem_limit_bytes=48 << 20
        ),
        name="block",
    )(
        in_hbm(latents.reshape(2, ROWS * W, C)),
        lengths,
        in_hbm(context),
        in_hbm(gain_first),
        in_hbm(gain_second),
        in_hbm(attn_gain),
        in_hbm(conv_first.reshape(3, 3 * C, C)),
        in_hbm(conv_second.reshape(3, 3 * C, C)),
        in_hbm(time_weight.reshape(3 * C, C)),
        in_hbm(w_qkv),
        in_hbm(w_out),
    )
    return result.reshape(2, ROWS, W, C)


def solution(mesh):
    placed = (P("clip", "tile", None, None), P("clip"), P(), P(), P(), P(), P(), P(), P(), P(), P())
    return jax.shard_map(
        local, mesh=mesh, in_specs=placed, out_specs=P("clip", "tile", None, None), check_vma=False
    )
```

```python
import jax
import jax.numpy as jnp
from jax import lax
from jax.experimental import pallas as pl
from jax.experimental.pallas import tpu as pltpu
from jax.sharding import PartitionSpec as P

MESH = pl.DeviceIdType.MESH
F32 = jnp.float32
BF16 = jnp.bfloat16

C = 320
HEAD_DIM = 64
HEADS = 5
GROUP_WIDTH = 10
H = 40
W = 64
ROWS = 5
CLIPS = 32
TILES = 8
COUNT = H * W * GROUP_WIDTH
EPS = 1e-05
MASKED = -1e30
DEAD = 1e30
DEAD_LIMIT = 1e20
CHUNKS = ((1, 2), (3, 0, 4))
STARTS = (0, 2)


def wrap(value, size):
    return jnp.where(value >= size, value - size, value)


def dot(a, b):
    return jnp.dot(a, b, preferred_element_type=F32)


def silu(y):
    half = 0.5 * y
    return half + half * jnp.tanh(half)


def rounded(v):
    return v.astype(BF16).astype(F32)


def channel_sums(frames):
    sums = [jnp.sum(v, axis=0, keepdims=True) for v in frames]
    squares = [jnp.sum(v * v, axis=0, keepdims=True) for v in frames]
    return jnp.concatenate(sums + squares, axis=0)


def kernel(
    lat_hbm, length_hbm, context_hbm, gain_one_hbm, gain_two_hbm, gain_attn_hbm,
    w_one_hbm, w_two_hbm, w_time_hbm, w_qkv_hbm, w_out_hbm,
    out,
    lat, length, context, gain_one, gain_two, gain_attn, w_one, w_two, w_time, w_qkv, w_out,
    taps, hid, halo_send, halo, member, stat_send, stat_recv, packed, qkv, masks,
    send_0, send_1, recv_0, recv_1, back_send_0, back_send_1, back_recv_0, back_recv_1,
    load_sem, halo_send_sem, halo_recv_sem, stat_send_sem, stat_recv_sem,
    a2a_send_sem, a2a_recv_sem,
):
    clip = lax.axis_index("clip")
    tile = lax.axis_index("tile")
    tile_up, tile_down = wrap(tile + TILES - 1, TILES), wrap(tile + 1, TILES)

    loads = [
        pltpu.make_async_copy(source, target, load_sem.at[i])
        for i, (source, target) in enumerate(
            (
                (lat_hbm, lat),
                (length_hbm, length),
                (context_hbm, context),
                (gain_one_hbm, gain_one),
                (gain_two_hbm, gain_two),
                (gain_attn_hbm, gain_attn),
                (w_one_hbm, w_one),
                (w_two_hbm, w_two),
                (w_time_hbm, w_time),
                (w_qkv_hbm, w_qkv),
                (w_out_hbm, w_out),
            )
        )
    ]
    for load in loads:
        load.start()

    barrier = pltpu.get_barrier_semaphore()

    for i in range(1, CLIPS):
        pl.semaphore_signal(
            barrier, inc=1, device_id={"clip": wrap(clip + i, CLIPS)}, device_id_type=MESH
        )
    for i in range(1, TILES):
        pl.semaphore_signal(
            barrier, inc=1, device_id={"tile": wrap(tile + i, TILES)}, device_id_type=MESH
        )

    rows = lax.broadcasted_iota(jnp.int32, (C, C), 0)
    cols = lax.broadcasted_iota(jnp.int32, (C, C), 1)
    member[...] = jnp.where(((rows * 6554) >> 16) == ((cols * 6554) >> 16), 1.0, 0.0).astype(BF16)

    def pack_halo(phase, source):
        for way, start in enumerate(((ROWS - 1) * W, 0)):
            span = pl.ds(start, W)
            for f in range(2):
                halo_send[phase, way, 2 * f] = source[f, span, 0:128]
                halo_send[phase, way, 2 * f + 1] = source[f, span, 128:256]
            halo_send[phase, way, 4] = jnp.concatenate(
                [source[0, span, 256:320], source[1, span, 256:320]], axis=1
            )

    for load in loads[:6]:
        load.wait()
    pack_halo(0, lat)
    first = channel_sums([lat[0].astype(F32), lat[1].astype(F32)])
    stat_send[0] = first
    pl.semaphore_wait(barrier, TILES - 1 + CLIPS - 1)

    def halo_copies(phase):
        return [
            pltpu.make_async_remote_copy(
                src_ref=halo_send.at[phase, way],
                dst_ref=halo.at[phase, way],
                send_sem=halo_send_sem.at[phase, way],
                recv_sem=halo_recv_sem.at[phase, way],
                device_id={"tile": peer},
                device_id_type=MESH,
            )
            for way, peer in enumerate((tile_down, tile_up))
        ]

    def stats_start(phase):
        for i in range(1, TILES):
            pltpu.make_async_remote_copy(
                src_ref=stat_send.at[phase],
                dst_ref=stat_recv.at[phase, tile],
                send_sem=stat_send_sem.at[phase],
                recv_sem=stat_recv_sem.at[phase],
                device_id={"tile": wrap(tile + i, TILES)},
                device_id_type=MESH,
            ).start()

    def batch_wait(buffer, count, sem):
        span = buffer.at[pl.ds(0, count)]
        pltpu.make_async_copy(span, span, sem).wait()

    def halo_start(phase):
        for copy in halo_copies(phase):
            copy.start()

    def halo_finish(phase):
        for copy in halo_copies(phase):
            copy.wait_recv()

    def stats_finish(phase, own, gain):
        stat_recv[phase, tile] = own

        batch_wait(stat_recv.at[phase], TILES - 1, stat_recv_sem.at[phase])
        total = stat_recv[phase, 0]
        for i in range(1, TILES):
            total = total + stat_recv[phase, i]
        top = total.astype(BF16)
        rest = total - top.astype(F32)
        mid = rest.astype(BF16)
        low = (rest - mid.astype(F32)).astype(BF16)
        grouped = dot(jnp.concatenate([top, mid, low], axis=0), member[...])
        grouped = ((grouped[8:12] + grouped[4:8]) + grouped[0:4]) * (1.0 / COUNT)
        centre = grouped[0:2]
        variance = grouped[2:4] - centre * centre
        scale = lax.rsqrt(variance + EPS) * gain[...].reshape(1, C)
        return scale, -centre * scale

    def exchange_drain(phase):
        batch_wait(stat_recv.at[phase], TILES - 1, stat_send_sem.at[phase])
        for copy in halo_copies(phase):
            copy.wait_send()

    def put_taps(f, start, rows, value, scale, shift, keep=None):
        a = silu(value.astype(F32) * scale + shift)
        if keep is not None:
            a = jnp.where(keep, a, 0.0)
        column = lax.broadcasted_iota(jnp.int32, (rows * W, C), 0) & (W - 1)
        before = jnp.where(column == 0, 0.0, pltpu.roll(a, 1, 0))
        after = jnp.where(column == W - 1, 0.0, pltpu.roll(a, rows * W - 1, 0))
        taps[f, pl.ds(start, rows * W), :] = jnp.concatenate(
            [before.astype(BF16), a.astype(BF16), after.astype(BF16)], axis=1
        )

    def fill_own(source, scale, shift):
        for f in range(2):
            put_taps(f, W, ROWS, source[f], scale[f : f + 1], shift[f : f + 1])

    def fill_edges(phase, scale, shift):
        for way, (start, keep) in enumerate(((0, tile > 0), ((ROWS + 1) * W, tile < TILES - 1))):
            for f in range(2):
                value = jnp.concatenate(
                    [
                        halo[phase, way, 2 * f],
                        halo[phase, way, 2 * f + 1],
                        halo[phase, way, 4][:, f * 64 : (f + 1) * 64],
                    ],
                    axis=1,
                )
                put_taps(f, start, 1, value, scale[f : f + 1], shift[f : f + 1], keep)

    def convolve(chunk, weights):
        total = None
        for a in range(3):
            lines = [
                taps[f, pl.ds((row + a) * W, W), :] for row in CHUNKS[chunk] for f in range(2)
            ]
            term = dot(jnp.concatenate(lines, axis=0), weights[a])
            total = term if total is None else total + term
        return total

    def first_convolution(chunk):
        value = convolve(chunk, w_one).astype(BF16)
        sums = []
        for q, row in enumerate(CHUNKS[chunk]):
            for f in range(2):
                hid[f, pl.ds(row * W, W), :] = value[(2 * q + f) * W : (2 * q + f + 1) * W]
        wide = value.astype(F32)
        for f in range(2):
            parts = [wide[(2 * q + f) * W : (2 * q + f + 1) * W] for q in range(len(CHUNKS[chunk]))]
            sums.append(jnp.concatenate(parts, axis=0))
        return channel_sums(sums)

    stats_start(0)
    halo_start(0)
    for load in loads[6:]:
        load.wait()
    for i in range(3):
        qkv[i] = w_qkv[:, i * C : (i + 1) * C]
    scale, shift = stats_finish(0, first, gain_one)
    fill_own(lat, scale, shift)
    second = first_convolution(0)
    halo_finish(0)
    fill_edges(0, scale, shift)
    second = second + first_convolution(1)
    stat_send[1] = second
    pack_halo(1, hid)

    stats_start(1)
    halo_start(1)
    exchange_drain(0)
    scale, shift = stats_finish(1, second, gain_two)
    fill_own(hid, scale, shift)

    def pack_row(r, value):
        base = r * 10 * CLIPS
        packed[pl.ds(base, 128), :] = value[:, 0:128]
        packed[pl.ds(base + 128, 128), :] = value[:, 128:256]
        packed[pl.ds(base + 256, 64), :] = jnp.concatenate(
            [value[0:64, 256:320], value[64:128, 256:320]], axis=1
        )

    def a2a_start(way, chunk, source, target):
        depth = len(CHUNKS[chunk]) * 10
        base = STARTS[chunk] * 10 * CLIPS
        block = packed[pl.ds(base, depth * CLIPS), :].reshape(depth, CLIPS, 128)
        source[...] = jnp.swapaxes(block, 0, 1).astype(BF16).reshape(CLIPS, depth // 2, 2, 128)
        target[clip] = source[clip]
        for i in range(1, CLIPS):
            peer = wrap(clip + i, CLIPS)
            pltpu.make_async_remote_copy(
                src_ref=source.at[peer],
                dst_ref=target.at[clip],
                send_sem=a2a_send_sem.at[way, chunk],
                recv_sem=a2a_recv_sem.at[way, chunk],
                device_id={"clip": peer},
                device_id_type=MESH,
            ).start()

    def a2a_finish(way, chunk, source, target):
        batch_wait(target, CLIPS - 1, a2a_recv_sem.at[way, chunk])
        wide = target[...].reshape(CLIPS, len(CHUNKS[chunk]) * 10, 128).astype(F32)
        block = jnp.swapaxes(wide, 0, 1)
        return [unpack_row(block[q * 10 : q * 10 + 10]) for q in range(len(CHUNKS[chunk]))]

    def a2a_drain(way, chunk, source, target):
        batch_wait(source, CLIPS - 1, a2a_send_sem.at[way, chunk])

    def unpack_row(block):
        left, middle = block[0:4].reshape(128, 128), block[4:8].reshape(128, 128)
        tail = block[8:10].reshape(64, 128)
        right = jnp.concatenate([tail, pltpu.roll(tail, 64, 1)], axis=0)
        return jnp.concatenate([left, middle, right[:, 0:64]], axis=1)

    one_live = length[0] == 1
    sends, recvs = (send_0, send_1), (recv_0, recv_1)
    back_sends, back_recvs = (back_send_0, back_send_1), (back_recv_0, back_recv_1)

    for chunk in range(2):
        if chunk == 1:
            halo_finish(1)
            fill_edges(1, scale, shift)
        total = convolve(chunk, w_two)
        for q, row in enumerate(CHUNKS[chunk]):
            halves = []
            for f in range(2):
                span = slice((2 * q + f) * W, (2 * q + f + 1) * W)
                value = lat[f, pl.ds(row * W, W), :].astype(F32) + total[span]
                halves.append(jnp.where(one_live, DEAD, value) if f == 1 else value)
            pack_row(STARTS[chunk] + q, jnp.concatenate(halves, axis=0))
        a2a_start(0, chunk, sends[chunk], recvs[chunk])

    exchange_drain(1)

    lane = lax.broadcasted_iota(jnp.int32, (128, 128), 1)
    line = lax.broadcasted_iota(jnp.int32, (128, 128), 0)
    lane_clip, lane_cell, lane_slot = lane & 31, (lane >> 5) & 1, lane >> 6
    line_clip, line_cell = line & 31, (line >> 5) & 1
    lane_frame = lane_clip * 2 + lane_slot
    shared = jnp.zeros((128, 128), F32)
    for j in range(8):
        shared = shared + jnp.where(lane_frame == context[j], 1.0, 0.0)
    low_half = lane < HEAD_DIM
    clip_row = lax.broadcasted_iota(jnp.int32, (CLIPS, C), 0)

    for chunk in range(2):
        rows = len(CHUNKS[chunk])
        blocks = a2a_finish(0, chunk, sends[chunk], recvs[chunk])
        if chunk == 0:
            dead = jnp.broadcast_to(blocks[0][64:96, 0:1], (CLIPS, 128)) > DEAD_LIMIT
            dead_wide = jnp.broadcast_to(blocks[0][64:96, 0:1], (CLIPS, C)) > DEAD_LIMIT
            dead_f = jnp.where(dead, 1.0, 0.0)
            dead_lane = jnp.sum(
                jnp.where(
                    lax.broadcasted_iota(jnp.int32, (CLIPS, 128), 0)
                    == (lax.broadcasted_iota(jnp.int32, (CLIPS, 128), 1) & 31),
                    dead_f,
                    0.0,
                ),
                axis=0,
                keepdims=True,
            )
            live_key = 1.0 - jnp.where(lane_slot == 1, jnp.broadcast_to(dead_lane, (128, 128)), 0.0)
            weight = jnp.where(
                lane_cell == line_cell,
                jnp.where(lane_clip == line_clip, live_key, 0.0) + shared,
                0.0,
            )
            masks[0] = weight
            masks[1] = jnp.where(weight > 0.0, 0.0, MASKED)

        sources = []
        for q in range(rows):
            x = jnp.where(blocks[q] > DEAD_LIMIT, 0.0, blocks[q])
            sources.append(x)
            moving = rounded(silu(x))
            before, after = [None] * 4, [None] * 4
            for cell in range(2):
                m0 = moving[cell * 32 : cell * 32 + 32]
                m1 = moving[64 + cell * 32 : 96 + cell * 32]
                final = jnp.where(dead_wide, m0, m1)
                prior = jnp.where(clip_row == 0, 0.0, pltpu.roll(final, 1, 0))
                later = jnp.where(clip_row == CLIPS - 1, 0.0, pltpu.roll(m0, CLIPS - 1, 0))
                before[cell], before[2 + cell] = prior, m0
                after[cell], after[2 + cell] = jnp.where(dead_wide, later, m1), later
            taps[0, pl.ds(q * 128, 128), :] = jnp.concatenate(
                [
                    jnp.concatenate(before, axis=0).astype(BF16),
                    moving.astype(BF16),
                    jnp.concatenate(after, axis=0).astype(BF16),
                ],
                axis=1,
            )
        source = jnp.concatenate(sources, axis=0)
        res_two = rounded(source + dot(taps[0, pl.ds(0, rows * 128), :], w_time[...]))
        centre = jnp.mean(res_two, axis=1, keepdims=True)
        offset = res_two - centre
        variance = jnp.mean(offset * offset, axis=1, keepdims=True)
        normed = (offset * lax.rsqrt(variance + EPS) * gain_attn[...].reshape(1, C)).astype(BF16)
        q_all = (dot(normed, qkv[0]) * (HEAD_DIM**-0.5)).astype(BF16)
        k_all = dot(normed, qkv[1]).astype(BF16)
        v_all = dot(normed, qkv[2]).astype(BF16)
        zero = jnp.zeros((128, 128), BF16)
        attended = []
        for q in range(rows):
            span = slice(q * 128, (q + 1) * 128)
            pieces = []
            for pair in range(2):
                cols = slice(pair * 128, (pair + 1) * 128)
                queries, keys, values = q_all[span, cols], k_all[span, cols], v_all[span, cols]
                keys2 = jnp.concatenate(
                    [jnp.where(low_half, keys, zero), jnp.where(low_half, zero, keys)], axis=0
                )
                values2 = jnp.concatenate(
                    [jnp.where(low_half, values, zero), jnp.where(low_half, zero, values)], axis=0
                )
                scores = lax.dot_general(
                    queries, keys2, (((1,), (1,)), ((), ())), preferred_element_type=F32
                )
                grown, norms = [], []
                for i in range(2):
                    part = scores[:, i * 128 : (i + 1) * 128] + masks[1]
                    part = jnp.exp(part - jnp.max(part, axis=1, keepdims=True)) * masks[0]
                    norms.append(jnp.broadcast_to(jnp.sum(part, axis=1, keepdims=True), (128, 128)))
                    grown.append(part.astype(BF16))
                norm = jnp.where(low_half, norms[0], norms[1])
                grown = jnp.concatenate(grown, axis=1)
                pieces.append((dot(grown, values2) / norm).astype(BF16))
            cols = slice(256, 320)
            scores = lax.dot_general(
                q_all[span, cols], k_all[span, cols], (((1,), (1,)), ((), ())),
                preferred_element_type=F32,
            )
            scores = scores + masks[1]
            grown = jnp.exp(scores - jnp.max(scores, axis=1, keepdims=True)) * masks[0]
            norm = jnp.sum(grown, axis=1, keepdims=True)
            pieces.append((dot(grown.astype(BF16), v_all[span, cols]) / norm).astype(BF16))
            attended.append(jnp.concatenate(pieces, axis=1))
        result = res_two + dot(jnp.concatenate(attended, axis=0), w_out[...])
        for q in range(rows):
            block = result[q * 128 : (q + 1) * 128]
            parts = [block[0:64]]
            for cell in range(2):
                parts.append(jnp.where(dead_wide, 0.0, block[64 + cell * 32 : 96 + cell * 32]))
            pack_row(STARTS[chunk] + q, jnp.concatenate(parts, axis=0))
        a2a_start(1, chunk, back_sends[chunk], back_recvs[chunk])

    for chunk in range(2):
        a2a_drain(0, chunk, sends[chunk], recvs[chunk])
    for chunk in range(2):
        blocks = a2a_finish(1, chunk, back_sends[chunk], back_recvs[chunk])
        for q, row in enumerate(CHUNKS[chunk]):
            for f in range(2):
                out[f, pl.ds(row * W, W), :] = blocks[q][f * 64 : (f + 1) * 64].astype(BF16)
    for chunk in range(2):
        a2a_drain(1, chunk, back_sends[chunk], back_recvs[chunk])


def in_hbm(x):
    return pltpu.with_memory_space_constraint(x, pltpu.HBM)


def local(
    latents, lengths, context, gain_first, conv_first, gain_second, conv_second,
    time_weight, attn_gain, w_qkv, w_out,
):
    vmem = pl.BlockSpec(memory_space=pltpu.VMEM)
    hbm = pl.BlockSpec(memory_space=pltpu.HBM)

    def messages(chunk):
        return pltpu.VMEM((CLIPS, len(CHUNKS[chunk]) * 5, 2, 128), BF16)

    result = pl.pallas_call(
        kernel,
        out_shape=jax.ShapeDtypeStruct((2, ROWS * W, C), BF16),
        in_specs=[hbm] * 11,
        out_specs=vmem,
        scratch_shapes=[
            pltpu.VMEM((2, ROWS * W, C), BF16),
            pltpu.SMEM((1,), jnp.int32),
            pltpu.SMEM((8,), jnp.int32),
            pltpu.VMEM((C,), F32),
            pltpu.VMEM((C,), F32),
            pltpu.VMEM((C,), F32),
            pltpu.VMEM((3, 3 * C, C), BF16),
            pltpu.VMEM((3, 3 * C, C), BF16),
            pltpu.VMEM((3 * C, C), BF16),
            pltpu.VMEM((C, 3 * C), BF16),
            pltpu.VMEM((C, C), BF16),
            pltpu.VMEM((2, (ROWS + 2) * W, 3 * C), BF16),
            pltpu.VMEM((2, ROWS * W, C), BF16),
            pltpu.VMEM((2, 2, 5, W, 128), BF16),
            pltpu.VMEM((2, 2, 5, W, 128), BF16),
            pltpu.VMEM((C, C), BF16),
            pltpu.VMEM((2, 4, C), F32),
            pltpu.VMEM((2, TILES, 4, C), F32),
            pltpu.VMEM((ROWS * 10 * CLIPS, 128), F32),
            pltpu.VMEM((3, C, C), BF16),
            pltpu.VMEM((2, 128, 128), F32),
            messages(0), messages(1), messages(0), messages(1),
            messages(0), messages(1), messages(0), messages(1),
            pltpu.SemaphoreType.DMA((11,)),
            pltpu.SemaphoreType.DMA((2, 2)),
            pltpu.SemaphoreType.DMA((2, 2)),
            pltpu.SemaphoreType.DMA((2,)),
            pltpu.SemaphoreType.DMA((2,)),
            pltpu.SemaphoreType.DMA((2, 2)),
            pltpu.SemaphoreType.DMA((2, 2)),
        ],
        compiler_params=pltpu.CompilerParams(
            collective_id=0, has_side_effects=True, vmem_limit_bytes=48 << 20
        ),
        name="block",
    )(
        in_hbm(latents.reshape(2, ROWS * W, C)),
        lengths,
        in_hbm(context),
        in_hbm(gain_first),
        in_hbm(gain_second),
        in_hbm(attn_gain),
        in_hbm(conv_first.reshape(3, 3 * C, C)),
        in_hbm(conv_second.reshape(3, 3 * C, C)),
        in_hbm(time_weight.reshape(3 * C, C)),
        in_hbm(w_qkv),
        in_hbm(w_out),
    )
    return result.reshape(2, ROWS, W, C)


def solution(mesh):
    placed = (P("clip", "tile", None, None), P("clip"), P(), P(), P(), P(), P(), P(), P(), P(), P())
    return jax.shard_map(
        local, mesh=mesh, in_specs=placed, out_specs=P("clip", "tile", None, None), check_vma=False
    )
```
